32 devices in a mesh: grp: 4 (over y, x), blk: 8 (over z, core).
Axes of the slice: x: 2, y: 2, z: 4, core: 2. Of those that a mesh axis runs over, the one named last changes fastest.
Arguments:
- queries: bfloat16 [4096, 1024], P(('grp', 'blk')), may hold values from -8 to 8
- key_rows: bfloat16 [4096, 128], P(('grp', 'blk')), may hold values from -8 to 8
- values: bfloat16 [4096, 128], P(('grp', 'blk')), may hold values from -6 to 6
- out_grad: bfloat16 [4096, 1024], P(('grp', 'blk')), may hold values from -6 to 6
- span_order: int32 [8], replicated, may hold values from 0 to 7, each once
Outputs:
- attended: bfloat16 [4096, 1024], P(('grp', 'blk'))
- grad_queries: bfloat16 [4096, 1024], P(('grp', 'blk'))
- grad_keys: bfloat16 [4096, 128], P(('grp', 'blk'))
- grad_values: bfloat16 [4096, 128], P(('grp', 'blk'))
The draws below stay inside these ranges and needn't reach their ends.
Inputs may be any that keep to these rules, and one draw needn't show every extreme that they name: `span_order`: a permutation of 0 to 7.
All inputs are finite; a program needn't handle non-finite values.
Results may differ from the reference program's by a relative error of at most 0.015.
Values may be sent and summed in bfloat16 or wider, within the bound.
No kernel may reach another device: no remote copies, remote signals or barrier semaphores. Data moves between devices by JAX's collectives and lax.ppermute only.
A program may use at most 64 MiB of HBM per device.

```python
import math
import jax
import jax.numpy as jnp
from jax import lax

GROUP = 8
HEAD = 128
ROWS = 128
TOKENS = 4096
N_GRP = 4
N_BLK = 8


def base_values(key, columns):
    return jnp.clip(jax.random.normal(key, (TOKENS, columns)), -4.0, 4.0)


def draw_queries(key, part):
    values_now = base_values(jax.random.fold_in(key, 11), GROUP * HEAD)
    return values_now.astype(jnp.bfloat16)


def draw_key_rows(key, part):
    values_now = base_values(jax.random.fold_in(key, 13), HEAD)
    return values_now.astype(jnp.bfloat16)


def levels(rng, extent, shards, smallest, top_value):
    def one(position, blocks):
        steps = jax.random.uniform(jax.random.fold_in(jax.random.fold_in(rng, 6), position), (blocks,), jnp.float32, smallest / len(shards), top_value / len(shards))
        return jnp.repeat(jnp.exp(steps), extent[position] // blocks).reshape((-1,) + (1,) * (len(extent) - position - 1))

    factor_of = one(*shards[0])
    for cut in shards[1:]:
        factor_of = factor_of * one(*cut)
    return factor_of


def bell_draw(stream_key, extent, scale, most, cuts=(), kind=jnp.bfloat16):
    result = scale * jax.random.normal(stream_key, extent, jnp.float32)
    if cuts:
        result = result * levels(stream_key, extent, cuts, -0.22, 0.18)
    return jnp.clip(result, -most, most).astype(kind)


def setup_inputs(seed: int = 0) -> dict:
    streams_of = jax.random.split(jax.random.key(seed), 6)
    return {
        "queries": draw_queries(jax.random.fold_in(streams_of[5], 71), 0),
        "key_rows": draw_key_rows(jax.random.fold_in(streams_of[5], 71), 0),
        "values": bell_draw(streams_of[2], (TOKENS, HEAD), 1.0, 6.0, ((0, 32),)),
        "out_grad": bell_draw(streams_of[3], (TOKENS, GROUP * HEAD), 1.0, 6.0, ((0, 32),)),
        "span_order": jax.random.permutation(streams_of[4], N_BLK).astype(jnp.int32),
    }


NEG_FILL = -1e+30

def rounded(matrix):
    return lax.optimization_barrier(matrix.astype(jnp.bfloat16)).astype(jnp.float32)

def token_positions(span_order):
    halfway = N_GRP // 2
    grp_ids = jnp.arange(N_GRP, dtype=jnp.int32)[:, None, None]
    lead_part = span_order.astype(jnp.int32)[None, :, None]
    section = jnp.where(grp_ids < halfway, lead_part, 2 * N_BLK - 1 - lead_part)
    inside = jnp.arange(ROWS, dtype=jnp.int32)[None, None, :]
    return section * (halfway * ROWS) + grp_ids % halfway * ROWS + inside

def block_pass(query_blk, grad_blk, query_pos, kv_rows, key_pos):
    factor = 1.0 / math.sqrt(HEAD)
    highest = lax.Precision.HIGHEST
    query_count = query_blk.shape[0]
    query_heads = query_blk.astype(jnp.float32).reshape(query_count, GROUP, HEAD)
    grad_heads = grad_blk.astype(jnp.float32).reshape(query_count, GROUP, HEAD)
    key_head = kv_rows[:, :HEAD].astype(jnp.float32)
    value_head = kv_rows[:, HEAD:].astype(jnp.float32)
    raw_scores = jnp.einsum('qhd,kd->hqk', query_heads, key_head, precision=highest) * factor
    visible = (key_pos[None, :] <= query_pos[:, None])[None, :, :]
    scores = jnp.where(visible, raw_scores, NEG_FILL)
    row_top = lax.optimization_barrier(jnp.max(scores, axis=2, keepdims=True))
    weights = jnp.where(visible, jnp.exp(scores - row_top), 0.0)
    row_total = lax.optimization_barrier(jnp.sum(weights, axis=2, keepdims=True))
    blended = jnp.einsum('hqk,kd->hqd', rounded(weights), value_head, precision=highest)
    out_heads = rounded(blended / row_total)
    row_delta = lax.optimization_barrier(jnp.sum(jnp.transpose(grad_heads, (1, 0, 2)) * out_heads, axis=2, keepdims=True))
    normed = weights / row_total
    value_grad = jnp.einsum('hqk,qhd->kd', rounded(normed), grad_heads, precision=highest)
    prob_grad = jnp.einsum('qhd,kd->hqk', grad_heads, value_head, precision=highest)
    score_grad = rounded(normed * (prob_grad - row_delta))
    query_grad = factor * jnp.einsum('hqk,kd->qhd', score_grad, key_head, precision=highest)
    key_grad = factor * jnp.einsum('hqk,qhd->kd', score_grad, query_heads, precision=highest)
    out_rows = jnp.transpose(out_heads, (1, 0, 2)).reshape(query_count, GROUP * HEAD).astype(jnp.bfloat16)
    query_rows = query_grad.reshape(query_count, GROUP * HEAD).astype(jnp.bfloat16)
    return (out_rows, query_rows, jnp.concatenate([key_grad, value_grad], axis=1))

def reference(queries, key_rows, values, out_grad, span_order):
    width = GROUP * HEAD
    places = token_positions(span_order)
    query_grid = queries.reshape(N_GRP, N_BLK, ROWS, width)
    grad_grid = out_grad.reshape(N_GRP, N_BLK, ROWS, width)
    pair_grid = jnp.concatenate([key_rows, values], axis=1).reshape(N_GRP, N_BLK, ROWS, 2 * HEAD)

    def column(grid, blk_id):
        picked = lax.dynamic_index_in_dim(grid, blk_id, 1, keepdims=False)
        return picked.reshape((N_GRP * ROWS,) + grid.shape[3:])

    def one_block(blk_id):
        nearby = [(blk_id + N_BLK - 1) % N_BLK, blk_id, (blk_id + 1) % N_BLK]
        kv_all = jnp.concatenate([column(pair_grid, neighbor) for neighbor in nearby], axis=0)
        key_pos = jnp.concatenate([column(places, neighbor) for neighbor in nearby], axis=0)
        out_rows, query_rows, kv_grad = block_pass(column(query_grid, blk_id), column(grad_grid, blk_id), column(places, blk_id), kv_all, key_pos)
        return (out_rows, query_rows, kv_grad.reshape(3, N_GRP * ROWS, 2 * HEAD))
    out_all, query_all, kv_parts = lax.map(one_block, jnp.arange(N_BLK, dtype=jnp.int32))
    kv_total = kv_parts[:, 1] + jnp.roll(kv_parts[:, 0], -1, axis=0) + jnp.roll(kv_parts[:, 2], 1, axis=0)

    def storage(stacked):
        breadth = stacked.shape[-1]
        return jnp.transpose(stacked.reshape(N_BLK, N_GRP, ROWS, breadth), (1, 0, 2, 3)).reshape(N_GRP * N_BLK * ROWS, breadth)
    kv_flat = storage(kv_total)
    return (storage(out_all), storage(query_all), kv_flat[:, :HEAD].astype(jnp.bfloat16), kv_flat[:, HEAD:].astype(jnp.bfloat16))
```

```python
import functools
import math

import jax
import jax.numpy as jnp
from jax import lax
from jax.experimental import pallas as pl
from jax.experimental.pallas import tpu as pltpu
from jax.sharding import PartitionSpec as P

HEAD = 128
NEG_FILL = -1e30
F32 = jnp.float32
BF16 = jnp.bfloat16
NT = (((1,), (1,)), ((), ()))


def dot(a, b):
    return jnp.dot(a, b, preferred_element_type=F32)


def dot_nt(a, b):
    return lax.dot_general(a, b, NT, preferred_element_type=F32)


def kernel(
    half, blk_count, span_ref, q_ref, go_ref, so, eo, sm, em, sf, ef,
    out_ref, gq_ref, gso, geo, gsm, gem, gsf, gef,
    qs, gos, got, w_ref, m_ref, m_run, l_run, o_run, gq_run, delta,
):
    rows, width = q_ref.shape
    heads = width // HEAD
    pair = 2 * rows
    pairs = heads // 2
    unit = so.shape[0]
    chunk = min(unit, 2 * rows)
    per_unit = unit // chunk
    factor = 1.0 / math.sqrt(HEAD)
    c2 = factor * math.log2(math.e)
    grp = lax.axis_index("grp")
    blk = lax.axis_index("blk")
    late = grp >= half
    idx = lax.rem(grp, half)
    even = lax.rem(blk, 2) == 0
    below = lax.rem(blk + blk_count - 1, blk_count)
    above = lax.rem(blk + 1, blk_count)
    mine = span_ref[blk]
    mate = span_ref[jnp.where(even, above, below)]
    off = span_ref[jnp.where(even, below, above)]
    see_m = late == (mate > mine)
    see_f = late == (off > mine)
    units = [
        (so, gso, None), (eo, geo, late), (sm, gsm, see_m), (em, gem, late), (sf, gsf, see_f), (ef, gef, late),
    ]

    for h in range(heads):
        qs[h * rows : (h + 1) * rows, :] = q_ref[:, h * HEAD : (h + 1) * HEAD]
        gh = go_ref[:, h * HEAD : (h + 1) * HEAD]
        gos[h * rows : (h + 1) * rows, :] = gh
        got[:, h * rows : (h + 1) * rows] = gh.T
    m_run[...] = jnp.full_like(m_run, NEG_FILL)
    l_run[...] = jnp.zeros_like(l_run)
    o_run[...] = jnp.zeros_like(o_run)
    gq_run[...] = jnp.zeros_like(gq_run)

    def forward(kv, slot, r0, mask):
        k = kv[r0 : r0 + chunk, :HEAD]
        vt = kv[r0 : r0 + chunk, HEAD:].T
        for p in range(pairs):
            cols = slice(p * pair, (p + 1) * pair)
            s = dot_nt(k, qs[cols, :]) * c2
            if mask is not None:
                s = jnp.where(mask, s, NEG_FILL)
            m_old = m_run[:, cols]
            m_new = jnp.maximum(m_old, jnp.max(s, axis=0, keepdims=True))
            w = jnp.exp2(s - m_new)
            if mask is not None:
                w = jnp.where(mask, w, 0.0)
            alpha = jnp.exp2(m_old - m_new)
            l_run[:, cols] = l_run[:, cols] * alpha + jnp.sum(w, axis=0, keepdims=True)
            w16 = w.astype(BF16)
            w_ref[slot, :, cols] = w16
            o_run[:, cols] = o_run[:, cols] * alpha + dot(vt, w16)
            m_run[:, cols] = m_new
            m_ref[slot, :, cols] = m_new

    def backward(kv, gkv, slot, r0):
        k = kv[r0 : r0 + chunk, :HEAD]
        kt = k.T
        v = kv[r0 : r0 + chunk, HEAD:]
        gk = jnp.zeros((chunk, HEAD), F32)
        gv = jnp.zeros((chunk, HEAD), F32)
        for p in range(pairs):
            cols = slice(p * pair, (p + 1) * pair)
            scale = jnp.exp2(m_ref[slot, :, cols] - m_run[:, cols]) * l_run[:, cols]
            prob = w_ref[slot, :, cols].astype(F32) * scale
            dp = dot_nt(v, gos[cols, :])
            ds = (prob * (dp - delta[:, cols])).astype(BF16)
            gv = gv + dot(prob.astype(BF16), gos[cols, :])
            gk = gk + dot(ds, qs[cols, :])
            gq_run[:, cols] = gq_run[:, cols] + dot(kt, ds)
        gkv[r0 : r0 + chunk, :HEAD] = (gk * factor).astype(BF16)
        gkv[r0 : r0 + chunk, HEAD:] = gv.astype(BF16)

    for i, (kv, gkv, see) in enumerate(units):
        for j in range(per_unit):
            slot, r0 = i * per_unit + j, j * chunk
            if see is None:
                row = lax.broadcasted_iota(jnp.int32, (chunk, pair), 0) + r0
                col = lax.broadcasted_iota(jnp.int32, (chunk, pair), 1)
                col = jnp.where(col >= rows, col - rows, col)
                mask = (row <= col) | ((row >= rows) & (row < (idx + 1) * rows))
                forward(kv, slot, r0, mask)
            else:
                pl.when(see)(functools.partial(forward, kv, slot, r0, None))

    for p in range(pairs):
        cols = slice(p * pair, (p + 1) * pair)
        inv = 1.0 / l_run[:, cols]
        l_run[:, cols] = inv
        o16 = (o_run[:, cols] * inv).astype(BF16)
        delta[:, cols] = jnp.sum(o16.astype(F32) * got[:, cols].astype(F32), axis=0, keepdims=True)
        for t in range(2):
            h = 2 * p + t
            out_ref[:, h * HEAD : (h + 1) * HEAD] = o16[:, t * rows : (t + 1) * rows].T

    for i, (kv, gkv, see) in enumerate(units):
        for j in range(per_unit):
            slot, r0 = i * per_unit + j, j * chunk
            if see is None:
                backward(kv, gkv, slot, r0)
            else:
                pl.when(see)(functools.partial(backward, kv, gkv, slot, r0))

                @pl.when(jnp.logical_not(see))
                def _():
                    gkv[r0 : r0 + chunk, :] = jnp.zeros((chunk, 2 * HEAD), BF16)

    for h in range(heads):
        g16 = (gq_run[:, h * rows : (h + 1) * rows] * factor).astype(BF16)
        gq_ref[:, h * HEAD : (h + 1) * HEAD] = g16.T


def attend(queries, grads, span_order, half, blk_count, units):
    rows, width = queries.shape
    unit = units[0].shape[0]
    chunk = min(unit, 2 * rows)
    slots = 6 * (unit // chunk)
    big = width // HEAD * rows
    vmem = pl.BlockSpec(memory_space=pltpu.VMEM)
    smem = pl.BlockSpec(memory_space=pltpu.SMEM)
    like = jax.ShapeDtypeStruct
    return pl.pallas_call(
        functools.partial(kernel, half, blk_count),
        out_shape=[like((rows, width), BF16)] * 2 + [like((unit, 2 * HEAD), BF16)] * 6,
        in_specs=[smem] + [vmem] * 8,
        out_specs=[vmem] * 8,
        scratch_shapes=[
            pltpu.VMEM((big, HEAD), BF16),
            pltpu.VMEM((big, HEAD), BF16),
            pltpu.VMEM((HEAD, big), BF16),
            pltpu.VMEM((slots, chunk, big), BF16),
            pltpu.VMEM((slots, 1, big), F32),
            pltpu.VMEM((1, big), F32),
            pltpu.VMEM((1, big), F32),
            pltpu.VMEM((HEAD, big), F32),
            pltpu.VMEM((HEAD, big), F32),
            pltpu.VMEM((1, big), F32),
        ],
        compiler_params=pltpu.CompilerParams(vmem_limit_bytes=40 << 20),
        name="attend",
    )(span_order, queries, grads, *units)


def body(queries, key_rows, values, out_grad, span_order):
    rows = queries.shape[0]
    grp_count = lax.axis_size("grp")
    blk_count = lax.axis_size("blk")
    half = grp_count // 2

    def send(block, grp_to, blk_to):
        route = []
        for g in range(grp_count):
            for b in range(blk_count):
                to = grp_to(g)
                if to is not None:
                    route.append((g * blk_count + b, to * blk_count + blk_to(b) % blk_count))
        return lax.ppermute(block, ("grp", "blk"), route)

    same = lambda i: i
    on_chip = lambda block: send(block, same, lambda b: b ^ 1)
    off_chip = lambda block: send(block, same, lambda b: b + 1 if b % 2 else b - 1)
    ring_up = lambda block: send(block, lambda g: g // half * half + (g + 1) % half, same)
    ring_down = lambda block: send(block, lambda g: g // half * half + (g - 1) % half, same)
    to_late = lambda block: send(block, lambda g: g + half if g < half else None, same)
    to_early = lambda block: send(block, lambda g: g - half if g >= half else None, same)

    own = jnp.concatenate([key_rows, values], axis=1)
    off = off_chip(own)
    parts = [jnp.concatenate([own, off], axis=0)]
    for _ in range(half - 1):
        parts.append(ring_up(parts[-1]))
    near = jnp.concatenate([p[:rows] for p in parts] + [p[rows:] for p in parts], axis=0)
    far = to_late(near)
    unit = half * rows
    so, sf, eo, ef = near[:unit], near[unit:], far[:unit], far[unit:]
    mate = on_chip(jnp.concatenate([so, eo], axis=0))
    sm, em = mate[:unit], mate[unit:]

    out, gq, gso, geo, gsm, gem, gsf, gef = attend(
        queries, out_grad, span_order, half, blk_count, [so, eo, sm, em, sf, ef]
    )

    add = lambda a, b: (a.astype(F32) + b.astype(F32)).astype(BF16)
    mate = on_chip(jnp.concatenate([gsm, gem], axis=0))
    gso, geo = add(gso, mate[:unit]), add(geo, mate[unit:])
    back = to_early(jnp.concatenate([geo, gef], axis=0))
    gso, gsf = add(gso, back[:unit]), add(gsf, back[unit:])
    slots = [
        jnp.concatenate([gso[s * rows : (s + 1) * rows], gsf[s * rows : (s + 1) * rows]], axis=0)
        for s in range(half)
    ]
    total = slots[-1]
    for s in range(half - 2, -1, -1):
        total = add(ring_down(total), slots[s])
    final = add(total[:rows], off_chip(total[rows:]))
    return (out, gq, final[:, :HEAD], final[:, HEAD:])


def solution(mesh):
    spec = P(("grp", "blk"), None)
    return jax.shard_map(
        body,
        mesh=mesh,
        in_specs=(spec, spec, spec, spec, P()),
        out_specs=(spec, spec, spec, spec),
        check_vma=False,
    )
```

```python
import functools
import math

import jax
import jax.numpy as jnp
from jax import lax
from jax.experimental import pallas as pl
from jax.experimental.pallas import tpu as pltpu
from jax.sharding import PartitionSpec as P

HEAD = 128
NEG_FILL = -1e30
F32 = jnp.float32
BF16 = jnp.bfloat16
NT = (((1,), (1,)), ((), ()))
FACTOR = 1.0 / math.sqrt(HEAD)
C2 = FACTOR * math.log2(math.e)
VMEM = pl.BlockSpec(memory_space=pltpu.VMEM)
SMEM = pl.BlockSpec(memory_space=pltpu.SMEM)


def dot(a, b):
    return jnp.dot(a, b, preferred_element_type=F32)


def dot_nt(a, b):
    return lax.dot_general(a, b, NT, preferred_element_type=F32)


def stacked(ref, p):
    return jnp.concatenate(
        [ref[:, 2 * p * HEAD : (2 * p + 1) * HEAD], ref[:, (2 * p + 1) * HEAD : (2 * p + 2) * HEAD]], axis=0
    )


def place(half, blk_count, span_ref):
    grp = lax.axis_index("grp")
    blk = lax.axis_index("blk")
    late = grp >= half
    even = lax.rem(blk, 2) == 0
    below = lax.rem(blk + blk_count - 1, blk_count)
    above = lax.rem(blk + 1, blk_count)
    mine = span_ref[blk]
    mate = span_ref[jnp.where(even, above, below)]
    off = span_ref[jnp.where(even, below, above)]
    return lax.rem(grp, half), late, late == (mate > mine), late == (off > mine)


def own_mask(chunk, rows, r0, idx):
    row = lax.broadcasted_iota(jnp.int32, (chunk, 2 * rows), 0) + r0
    col = lax.broadcasted_iota(jnp.int32, (chunk, 2 * rows), 1)
    col = jnp.where(col >= rows, col - rows, col)
    return (row <= col) | ((row >= rows) & (row < (idx + 1) * rows))


def visit(see, run):
    if see is None:
        run()
    else:
        pl.when(see)(run)


def forward_unit(q_ref, kv, o_run, m_run, l_run, idx):
    rows, width = q_ref.shape
    pair = 2 * rows
    chunk = min(kv.shape[0], 2 * rows)
    for r0 in range(0, kv.shape[0], chunk):
        k = kv[r0 : r0 + chunk, :HEAD]
        vt = kv[r0 : r0 + chunk, HEAD:].T
        mask = None if idx is None else own_mask(chunk, rows, r0, idx)
        for p in range(width // (2 * HEAD)):
            cols = slice(p * pair, (p + 1) * pair)
            s = dot_nt(k, stacked(q_ref, p)) * C2
            if mask is not None:
                s = jnp.where(mask, s, NEG_FILL)
            m_old = m_run[:, cols]
            m_new = jnp.maximum(m_old, jnp.max(s, axis=0, keepdims=True))
            w = jnp.exp2(s - m_new)
            if mask is not None:
                w = jnp.where(mask, w, 0.0)
            alpha = jnp.exp2(m_old - m_new)
            l_run[:, cols] = l_run[:, cols] * alpha + jnp.sum(w, axis=0, keepdims=True)
            o_run[:, cols] = o_run[:, cols] * alpha + dot(vt, w.astype(BF16))
            m_run[:, cols] = m_new


def near_kernel(half, blk_count, span_ref, q_ref, so, sm, sf, o_run, m_run, l_run):
    idx, late, see_m, see_f = place(half, blk_count, span_ref)
    m_run[...] = jnp.full_like(m_run, NEG_FILL)
    l_run[...] = jnp.zeros_like(l_run)
    o_run[...] = jnp.zeros_like(o_run)
    forward_unit(q_ref, so, o_run, m_run, l_run, idx)
    for kv, see in ((sm, see_m), (sf, see_f)):
        visit(see, functools.partial(forward_unit, q_ref, kv, o_run, m_run, l_run, None))


def far_kernel(
    half, blk_count, span_ref, q_ref, go_ref, eo, em, ef, o_in, m_in, l_in, out_ref, lse_ref, delta_ref, o_run, m_run, l_run
):
    idx, late, see_m, see_f = place(half, blk_count, span_ref)
    rows, width = q_ref.shape
    pair = 2 * rows
    o_run[...] = o_in[...]
    m_run[...] = m_in[...]
    l_run[...] = l_in[...]
    for kv in (eo, em, ef):
        visit(late, functools.partial(forward_unit, q_ref, kv, o_run, m_run, l_run, None))
    ones = jnp.ones((8, HEAD), BF16)
    for p in range(width // (2 * HEAD)):
        cols = slice(p * pair, (p + 1) * pair)
        total = l_run[:, cols]
        o16 = (o_run[:, cols] * (1.0 / total)).astype(BF16).T
        lse_ref[:, cols] = m_run[:, cols] + jnp.log2(total)
        out_ref[:, 2 * p * HEAD : (2 * p + 1) * HEAD] = o16[:rows]
        out_ref[:, (2 * p + 1) * HEAD : (2 * p + 2) * HEAD] = o16[rows:]
        prod = o16.astype(F32) * stacked(go_ref, p).astype(F32)
        high = prod.astype(BF16)
        rest = prod - high.astype(F32)
        mid = rest.astype(BF16)
        low = (rest - mid.astype(F32)).astype(BF16)
        delta_ref[:, cols] = (dot_nt(ones, high) + dot_nt(ones, mid) + dot_nt(ones, low))[:1]


def backward_unit(q_ref, go_ref, lse_ref, delta_ref, kv, gkv, gq_run, idx):
    rows, width = q_ref.shape
    pair = 2 * rows
    chunk = min(kv.shape[0], 2 * rows)
    for r0 in range(0, kv.shape[0], chunk):
        k = kv[r0 : r0 + chunk, :HEAD]
        kt = k.T
        v = kv[r0 : r0 + chunk, HEAD:]
        gk = jnp.zeros((chunk, HEAD), F32)
        gv = jnp.zeros((chunk, HEAD), F32)
        mask = None if idx is None else own_mask(chunk, rows, r0, idx)
        for p in range(width // (2 * HEAD)):
            cols = slice(p * pair, (p + 1) * pair)
            q2 = stacked(q_ref, p)
            g2 = stacked(go_ref, p)
            prob = jnp.exp2(dot_nt(k, q2) * C2 - lse_ref[:, cols])
            if mask is not None:
                prob = jnp.where(mask, prob, 0.0)
            dp = dot_nt(v, g2)
            ds = (prob * (dp - delta_ref[:, cols])).astype(BF16)
            gv = gv + dot(prob.astype(BF16), g2)
            gk = gk + dot(ds, q2)
            gq_run[:, cols] = gq_run[:, cols] + dot(kt, ds)
        gkv[r0 : r0 + chunk, :HEAD] = (gk * FACTOR).astype(BF16)
        gkv[r0 : r0 + chunk, HEAD:] = gv.astype(BF16)


def back_kernel(half, blk_count, which, span_ref, q_ref, go_ref, lse_ref, delta_ref, s_kv, e_kv, *refs):
    idx, late, see_m, see_f = place(half, blk_count, span_ref)
    rows, width = q_ref.shape
    if which == "off":
        gs, ge, gq_run = refs
        gq_run[...] = jnp.zeros_like(gq_run)
    elif which == "mate":
        gq_in, gs, ge, gq_run = refs
        gq_run[...] = gq_in[...]
    else:
        gq_in, gs, ge, gq_ref, gq_run = refs
        gq_run[...] = gq_in[...]
    see = {"off": see_f, "mate": see_m, "own": None}[which]
    for kv, gkv, shown, tri in ((e_kv, ge, late, None), (s_kv, gs, see, idx if which == "own" else None)):
        visit(
            shown,
            functools.partial(backward_unit, q_ref, go_ref, lse_ref, delta_ref, kv, gkv, gq_run, tri),
        )
        if shown is not None:

            @pl.when(jnp.logical_not(shown))
            def _(gkv=gkv):
                gkv[...] = jnp.zeros_like(gkv)

    if which == "own":
        for h in range(width // HEAD):
            g16 = (gq_run[:, h * rows : (h + 1) * rows] * FACTOR).astype(BF16)
            gq_ref[:, h * HEAD : (h + 1) * HEAD] = g16.T


def like(shape, dtype):
    return jax.ShapeDtypeStruct(shape, dtype)


def call(kernel, name, outs, scratch, units, args):
    rows, width = args[1].shape
    keys = sum(u.shape[0] for u in units)
    work = 2 * keys * rows * width
    return pl.pallas_call(
        kernel,
        out_shape=outs,
        in_specs=[SMEM] + [VMEM] * (len(args) - 1),
        out_specs=[VMEM] * len(outs),
        scratch_shapes=scratch,
        cost_estimate=pl.CostEstimate(flops=4 * work, bytes_accessed=4 * rows * width, transcendentals=work // 256),
        compiler_params=pltpu.CompilerParams(vmem_limit_bytes=24 << 20),
        name=name,
    )(*args)


def body(queries, key_rows, values, out_grad, span_order):
    rows, width = queries.shape
    grp_count = lax.axis_size("grp")
    blk_count = lax.axis_size("blk")
    half = grp_count // 2
    unit = half * rows
    big = width // HEAD * rows
    wide, line = like((HEAD, big), F32), like((1, big), F32)
    tile = like((unit, 2 * HEAD), BF16)
    full = like((rows, width), BF16)
    wide_s, line_s = pltpu.VMEM((HEAD, big), F32), pltpu.VMEM((1, big), F32)

    def send(block, grp_to, blk_to):
        route = []
        for g in range(grp_count):
            for b in range(blk_count):
                to = grp_to(g)
                if to is not None:
                    route.append((g * blk_count + b, to * blk_count + blk_to(b) % blk_count))
        return lax.ppermute(block, ("grp", "blk"), route)

    same = lambda i: i
    on_chip = lambda block: send(block, same, lambda b: b ^ 1)
    off_chip = lambda block: send(block, same, lambda b: b + 1 if b % 2 else b - 1)
    ring_up = lambda block: send(block, lambda g: g // half * half + (g + 1) % half, same)
    ring_down = lambda block: send(block, lambda g: g // half * half + (g - 1) % half, same)
    to_late = lambda block: send(block, lambda g: g + half if g < half else None, same)
    to_early = lambda block: send(block, lambda g: g - half if g >= half else None, same)

    def gathered(block):
        parts = [block]
        for _ in range(half - 1):
            parts.append(ring_up(parts[-1]))
        return jnp.concatenate(parts, axis=0)

    def scattered(block):
        slots = [block[s * rows : (s + 1) * rows] for s in range(half)]
        total = slots[-1]
        for s in range(half - 2, -1, -1):
            total = add(ring_down(total), slots[s])
        return total

    add = lambda a, b: (a.astype(F32) + b.astype(F32)).astype(BF16)
    own = jnp.concatenate([key_rows, values], axis=1)
    off = off_chip(own)
    so = gathered(own)
    sf = gathered(off)
    sm = on_chip(so)
    eo = to_late(so)
    ef = to_late(sf)
    em = on_chip(eo)

    o_run, m_run, l_run = call(
        functools.partial(near_kernel, half, blk_count), "near", [wide, line, line], [],
        [so, sm, sf], [span_order, queries, so, sm, sf],
    )
    out, lse, delta = call(
        functools.partial(far_kernel, half, blk_count), "far", [full, line, line], [wide_s, line_s, line_s],
        [eo, em, ef], [span_order, queries, out_grad, eo, em, ef, o_run, m_run, l_run],
    )

    state = [span_order, queries, out_grad, lse, delta]
    back = lambda which: functools.partial(back_kernel, half, blk_count, which)
    gsf, gef, gq = call(back("off"), "back_off", [tile, tile, wide], [], [sf, ef], state + [sf, ef])
    gsm, gem, gq = call(back("mate"), "back_mate", [tile, tile, wide], [], [sm, em], state + [sm, em, gq])
    gso, geo, gq = call(back("own"), "back_own", [tile, tile, full], [wide_s], [so, eo], state + [so, eo, gq])

    gsf = add(gsf, to_early(gef))
    total_f = scattered(gsf)
    ret_f = off_chip(total_f)
    mate = on_chip(jnp.concatenate([gsm, gem], axis=0))
    geo = add(geo, mate[unit:])
    gso = gso.astype(F32) + mate[:unit].astype(F32)
    gso = (gso + to_early(geo).astype(F32)).astype(BF16)
    final = add(scattered(gso), ret_f)
    return (out, gq, final[:, :HEAD], final[:, HEAD:])


def solution(mesh):
    spec = P(("grp", "blk"), None)
    return jax.shard_map(
        body,
        mesh=mesh,
        in_specs=(spec, spec, spec, spec, P()),
        out_specs=(spec, spec, spec, spec),
        check_vma=False,
    )
```

```python
import functools
import math

import jax
import jax.numpy as jnp
from jax import lax
from jax.experimental import pallas as pl
from jax.experimental.pallas import tpu as pltpu
from jax.sharding import PartitionSpec as P

HEAD = 128
NEG_FILL = -1e30
F32 = jnp.float32
BF16 = jnp.bfloat16
NT = (((1,), (1,)), ((), ()))
FACTOR = 1.0 / math.sqrt(HEAD)
C2 = FACTOR * math.log2(math.e)
VMEM = pl.BlockSpec(memory_space=pltpu.VMEM)
SMEM = pl.BlockSpec(memory_space=pltpu.SMEM)


def dot(a, b):
    return jnp.dot(a, b, preferred_element_type=F32)


def dot_nt(a, b):
    return lax.dot_general(a, b, NT, preferred_element_type=F32)


def place(half, blk_count, span_ref):
    grp = lax.axis_index("grp")
    blk = lax.axis_index("blk")
    late = grp >= half
    even = lax.rem(blk, 2) == 0
    below = lax.rem(blk + blk_count - 1, blk_count)
    above = lax.rem(blk + 1, blk_count)
    mine = span_ref[blk]
    mate = span_ref[jnp.where(even, above, below)]
    off = span_ref[jnp.where(even, below, above)]
    return lax.rem(grp, half), late, late == (mate > mine), late == (off > mine)


def own_mask(keys, rows, idx):
    row = lax.broadcasted_iota(jnp.int32, (keys, 2 * rows), 0)
    col = lax.broadcasted_iota(jnp.int32, (keys, 2 * rows), 1)
    col = jnp.where(col >= rows, col - rows, col)
    return (row <= col) | ((row >= rows) & (row < (idx + 1) * rows))


def visit(see, run):
    if see is None:
        run()
    else:
        pl.when(see)(run)


def attend_group(units, sees, mask, qs, m_in, m_ref, w_ref, s_ref, finish):
    keys = units[0].shape[0]
    big = qs.shape[0]
    pair = min(big, 2 * HEAD)
    ones = jnp.ones((16, keys), BF16)
    for c in range(0, big, pair):
        cols = slice(c, c + pair)
        top = m_in[:, cols] if m_in is not None else jnp.full((1, pair), NEG_FILL, F32)
        for u, (kv, see) in enumerate(zip(units, sees)):
            s = dot_nt(kv[:, :HEAD], qs[cols, :]) * C2
            if u == 0 and mask is not None:
                s = jnp.where(mask, s, NEG_FILL)
            s_ref[u, :, cols] = s
            peak = jnp.max(s, axis=0, keepdims=True)
            top = jnp.maximum(top, peak if see is None else jnp.where(see, peak, NEG_FILL))
        m_ref[:, cols] = top
    vt = jnp.concatenate([jnp.concatenate([kv[:, HEAD:].T, ones], axis=0) for kv in units], axis=1)
    for c in range(0, big, pair):
        cols = slice(c, c + pair)
        top = m_ref[:, cols]
        for u, see in enumerate(sees):
            base = top if see is None else jnp.where(see, top, -NEG_FILL)
            w_ref[u * keys : (u + 1) * keys, cols] = jnp.exp2(s_ref[u, :, cols] - base).astype(BF16)
        summed = dot(vt, w_ref[:, cols])
        finish(cols, summed[:HEAD], summed[HEAD : HEAD + 1])


def near_kernel(
    half, blk_count, span_ref, q_ref, go_ref, so, sm, sf, o_ref, m_ref, l_ref, w_ref, qs, gs, s_ref
):
    idx, late, see_m, see_f = place(half, blk_count, span_ref)
    rows, width = q_ref.shape
    for h in range(width // HEAD):
        qs[h * rows : (h + 1) * rows, :] = q_ref[:, h * HEAD : (h + 1) * HEAD]
        gs[h * rows : (h + 1) * rows, :] = go_ref[:, h * HEAD : (h + 1) * HEAD]

    def finish(cols, summed, total):
        o_ref[:, cols] = summed
        l_ref[:, cols] = total

    mask = own_mask(so.shape[0], rows, idx)
    attend_group((so, sm, sf), (None, see_m, see_f), mask, qs, None, m_ref, w_ref, s_ref, finish)


def far_kernel(
    half, blk_count, span_ref, qs, gs, eo, em, ef, o_in, m_in, l_in,
    out_ref, w_ref, near_ref, far_ref, delta_ref, o_run, m_run, l_run, s_ref,
):
    idx, late, see_m, see_f = place(half, blk_count, span_ref)
    rows = out_ref.shape[0]
    big = qs.shape[0]
    pair = 2 * rows

    @pl.when(late)
    def _():
        def finish(cols, summed, total):
            alpha = jnp.exp2(m_in[:, cols] - m_run[:, cols])
            o_run[:, cols] = o_in[:, cols] * alpha + summed
            l_run[:, cols] = l_in[:, cols] * alpha + total

        attend_group((eo, em, ef), (None,) * 3, None, qs, m_in, m_run, w_ref, s_ref, finish)

    @pl.when(jnp.logical_not(late))
    def _():
        o_run[...] = o_in[...]
        m_run[...] = m_in[...]
        l_run[...] = l_in[...]

    ones = jnp.ones((8, HEAD), BF16)
    for p in range(big // pair):
        cols = slice(p * pair, (p + 1) * pair)
        inv = 1.0 / l_run[:, cols]
        far_ref[:, cols] = inv
        near_ref[:, cols] = inv * jnp.exp2(m_in[:, cols] - m_run[:, cols])
        o16 = (o_run[:, cols] * inv).astype(BF16).T
        out_ref[:, 2 * p * HEAD : (2 * p + 1) * HEAD] = o16[:rows]
        out_ref[:, (2 * p + 1) * HEAD : (2 * p + 2) * HEAD] = o16[rows:]
        prod = o16.astype(F32) * gs[cols, :].astype(F32)
        high = prod.astype(BF16)
        low = (prod - high.astype(F32)).astype(BF16)
        delta_ref[:, cols] = (dot_nt(ones, high) + dot_nt(ones, low))[:1]


def backward_unit(qs, gs, w_ref, slot, scale_ref, delta_ref, kv, gkv, gq_run, first, p_ref, d_ref):
    keys = kv.shape[0]
    big = qs.shape[0]
    pair = min(big, 2 * HEAD)
    kt = kv[:, :HEAD].T
    for c in range(0, big, pair):
        cols = slice(c, c + pair)
        prob = w_ref[slot * keys : (slot + 1) * keys, cols].astype(F32) * scale_ref[:, cols]
        dp = dot_nt(kv[:, HEAD:], gs[cols, :])
        p_ref[:, cols] = prob.astype(BF16)
        d_ref[:, cols] = (prob * (dp - delta_ref[:, cols])).astype(BF16)
    gkv[:, :HEAD] = (dot(d_ref[...], qs[...]) * FACTOR).astype(BF16)
    gkv[:, HEAD:] = dot(p_ref[...], gs[...]).astype(BF16)
    gq_run[...] = first[...] + dot(kt, d_ref[...])


def back_kernel(half, blk_count, which, span_ref, qs, gs, nw, fw, near_ref, far_ref, delta_ref, s_kv, e_kv, *refs):
    idx, late, see_m, see_f = place(half, blk_count, span_ref)
    if which == "off":
        gs_out, ge_out, gq_run, ps, ds, pe, de = refs
        slot, see = 2, see_f
        gq_run[...] = jnp.zeros_like(gq_run)
        first = gq_run
    elif which == "mate":
        first, gs_out, ge_out, gq_run, ps, ds, pe, de = refs
        slot, see = 1, see_m
    else:
        first, gs_out, ge_out, gq_ref, gq_run, ps, ds, pe, de = refs
        slot, see = 0, None
    if which == "mate":

        @pl.when(jnp.logical_not(see))
        def _():
            gq_run[...] = first[...]

    visit(
        see,
        functools.partial(
            backward_unit, qs, gs, nw, slot, near_ref, delta_ref, s_kv, gs_out, gq_run, first, ps, ds
        ),
    )
    visit(
        late,
        functools.partial(
            backward_unit, qs, gs, fw, slot, far_ref, delta_ref, e_kv, ge_out, gq_run, gq_run, pe, de
        ),
    )
    for gkv, shown in ((gs_out, see), (ge_out, late)):
        if shown is not None:

            @pl.when(jnp.logical_not(shown))
            def _(gkv=gkv):
                gkv[...] = jnp.zeros_like(gkv)

    if which == "own":
        rows = gq_ref.shape[0]
        for h in range(qs.shape[0] // rows):
            g16 = (gq_run[:, h * rows : (h + 1) * rows] * FACTOR).astype(BF16)
            gq_ref[:, h * HEAD : (h + 1) * HEAD] = g16.T


def like(shape, dtype):
    return jax.ShapeDtypeStruct(shape, dtype)


def call(kernel, name, outs, scratch, units, args):
    rows, width = args[1].shape
    keys = sum(u.shape[0] for u in units)
    work = 2 * keys * rows * width
    return pl.pallas_call(
        kernel,
        out_shape=outs,
        in_specs=[SMEM] + [VMEM] * (len(args) - 1),
        out_specs=[VMEM] * len(outs),
        scratch_shapes=scratch,
        cost_estimate=pl.CostEstimate(flops=4 * work, bytes_accessed=4 * rows * width, transcendentals=work // 256),
        compiler_params=pltpu.CompilerParams(vmem_limit_bytes=30 << 20),
        name=name,
    )(*args)


def body(queries, key_rows, values, out_grad, span_order):
    rows, width = queries.shape
    grp_count = lax.axis_size("grp")
    blk_count = lax.axis_size("blk")
    half = grp_count // 2
    unit = half * rows
    big = width // HEAD * rows
    wide, line = like((HEAD, big), F32), like((1, big), F32)
    tile = like((unit, 2 * HEAD), BF16)
    full = like((rows, width), BF16)
    wide_s, line_s = pltpu.VMEM((HEAD, big), F32), pltpu.VMEM((1, big), F32)

    def send(block, grp_to, blk_to):
        route = []
        for g in range(grp_count):
            for b in range(blk_count):
                to = grp_to(g)
                if to is not None:
                    route.append((g * blk_count + b, to * blk_count + blk_to(b) % blk_count))
        return lax.ppermute(block, ("grp", "blk"), route)

    same = lambda i: i
    on_chip = lambda block: send(block, same, lambda b: b ^ 1)
    off_chip = lambda block: send(block, same, lambda b: b + 1 if b % 2 else b - 1)
    ring_up = lambda block: send(block, lambda g: g // half * half + (g + 1) % half, same)
    ring_down = lambda block: send(block, lambda g: g // half * half + (g - 1) % half, same)
    to_late = lambda block: send(block, lambda g: g + half if g < half else None, same)
    to_early = lambda block: send(block, lambda g: g - half if g >= half else None, same)

    def gathered(block):
        parts = [block]
        for _ in range(half - 1):
            parts.append(ring_up(parts[-1]))
        return jnp.concatenate(parts, axis=0)

    def scattered(block):
        slots = [block[s * rows : (s + 1) * rows] for s in range(half)]
        total = slots[-1]
        for s in range(half - 2, -1, -1):
            total = add(ring_down(total), slots[s])
        return total

    add = lambda a, b: (a.astype(F32) + b.astype(F32)).astype(BF16)
    own = jnp.concatenate([key_rows, values], axis=1)
    off = off_chip(own)
    so = gathered(own)
    sf = gathered(off)
    sm = on_chip(so)
    eo = to_late(so)
    ef = to_late(sf)
    em = on_chip(eo)

    stack = like((big, HEAD), BF16)
    weights = like((3 * unit, big), BF16)
    scores = pltpu.VMEM((3, unit, big), F32)
    o_run, m_run, l_run, nw, qs, gs = call(
        functools.partial(near_kernel, half, blk_count), "near", [wide, line, line, weights, stack, stack], [scores],
        [so, sm, sf], [span_order, queries, out_grad, so, sm, sf],
    )
    out, fw, near, far, delta = call(
        functools.partial(far_kernel, half, blk_count), "far", [full, weights, line, line, line],
        [wide_s, line_s, line_s, scores],
        [eo, em, ef], [span_order, qs, gs, eo, em, ef, o_run, m_run, l_run],
    )

    state = [span_order, qs, gs, nw, fw, near, far, delta]
    back = lambda which: functools.partial(back_kernel, half, blk_count, which)
    temp = [pltpu.VMEM((unit, big), BF16)] * 4
    gsf, gef, gq = call(back("off"), "back_off", [tile, tile, wide], temp, [sf, ef], state + [sf, ef])
    gsm, gem, gq = call(back("mate"), "back_mate", [tile, tile, wide], temp, [sm, em], state + [sm, em, gq])
    gso, geo, gq = call(back("own"), "back_own", [tile, tile, full], [wide_s] + temp, [so, eo], state + [so, eo, gq])

    gsf = add(gsf, to_early(gef))
    total_f = scattered(gsf)
    ret_f = off_chip(total_f)
    mate = on_chip(jnp.concatenate([gsm, gem], axis=0))
    geo = add(geo, mate[unit:])
    gso = gso.astype(F32) + mate[:unit].astype(F32)
    gso = (gso + to_early(geo).astype(F32)).astype(BF16)
    final = add(scattered(gso), ret_f)
    return (out, gq, final[:, :HEAD], final[:, HEAD:])


def solution(mesh):
    spec = P(("grp", "blk"), None)
    return jax.shard_map(
        body,
        mesh=mesh,
        in_specs=(spec, spec, spec, spec, P()),
        out_specs=(spec, spec, spec, spec),
        check_vma=False,
    )
```

```python
import functools
import math

import jax
import jax.numpy as jnp
from jax import lax
from jax.experimental import pallas as pl
from jax.experimental.pallas import tpu as pltpu
from jax.sharding import PartitionSpec as P


HEAD = 128
NEG_FILL = -1e30
F32 = jnp.float32
BF16 = jnp.bfloat16
NT = (((1,), (1,)), ((), ()))
FACTOR = 1.0 / math.sqrt(HEAD)
C2 = FACTOR * math.log2(math.e)
VMEM = pl.BlockSpec(memory_space=pltpu.VMEM)
SMEM = pl.BlockSpec(memory_space=pltpu.SMEM)


def dot(a, b):
    return jnp.dot(a, b, preferred_element_type=F32)


def dot_nt(a, b):
    return lax.dot_general(a, b, NT, preferred_element_type=F32)


def place(half, blk_count, span_ref):
    grp = lax.axis_index("grp")
    blk = lax.axis_index("blk")
    late = grp >= half
    even = lax.rem(blk, 2) == 0
    below = lax.rem(blk + blk_count - 1, blk_count)
    above = lax.rem(blk + 1, blk_count)
    mine = span_ref[blk]
    mate = span_ref[jnp.where(even, above, below)]
    off = span_ref[jnp.where(even, below, above)]
    return lax.rem(grp, half), late, late == (mate > mine), late == (off > mine)


def own_mask(keys, rows, idx):
    row = lax.broadcasted_iota(jnp.int32, (keys, 2 * rows), 0)
    col = lax.broadcasted_iota(jnp.int32, (keys, 2 * rows), 1)
    col = jnp.where(col >= rows, col - rows, col)
    return (row <= col) | ((row >= rows) & (row < (idx + 1) * rows))


def visit(see, run):
    if see is None:
        run()
    else:
        pl.when(see)(run)


def attend_group(units, sees, mask, qs, m_in, m_ref, w_ref, s_ref, finish):
    keys = units[0].shape[0]
    big = qs.shape[0]
    pair = min(big, 2 * HEAD)
    ones = jnp.ones((16, keys), BF16)
    for c in range(0, big, pair):
        cols = slice(c, c + pair)
        top = m_in[:, cols] if m_in is not None else jnp.full((1, pair), NEG_FILL, F32)
        for u, (kv, see) in enumerate(zip(units, sees)):
            s = dot_nt(kv[:, :HEAD], qs[cols, :]) * C2
            if u == 0 and mask is not None:
                s = jnp.where(mask, s, NEG_FILL)
            s_ref[u, :, cols] = s
            peak = jnp.max(s, axis=0, keepdims=True)
            top = jnp.maximum(top, peak if see is None else jnp.where(see, peak, NEG_FILL))
        m_ref[:, cols] = top
    vt = jnp.concatenate([jnp.concatenate([kv[:, HEAD:].T, ones], axis=0) for kv in units], axis=1)
    for c in range(0, big, pair):
        cols = slice(c, c + pair)
        top = m_ref[:, cols]
        for u, see in enumerate(sees):
            base = top if see is None else jnp.where(see, top, -NEG_FILL)
            w_ref[u * keys : (u + 1) * keys, cols] = jnp.exp2(s_ref[u, :, cols] - base).astype(BF16)
        summed = dot(vt, w_ref[:, cols])
        finish(cols, summed[:HEAD], summed[HEAD : HEAD + 1])


def near_kernel(
    half, blk_count, span_ref, q_ref, go_ref, so, sm, sf, o_ref, m_ref, l_ref, w_ref, qs, gs, s_ref
):
    idx, _, see_m, see_f = place(half, blk_count, span_ref)
    rows, width = q_ref.shape
    for h in range(width // HEAD):
        qs[h * rows : (h + 1) * rows, :] = q_ref[:, h * HEAD : (h + 1) * HEAD]
        gs[h * rows : (h + 1) * rows, :] = go_ref[:, h * HEAD : (h + 1) * HEAD]

    def finish(cols, summed, total):
        o_ref[:, cols] = summed
        l_ref[:, cols] = total

    mask = own_mask(so.shape[0], rows, idx)
    attend_group((so, sm, sf), (None, see_m, see_f), mask, qs, None, m_ref, w_ref, s_ref, finish)


def far_kernel(
    half, blk_count, span_ref, qs, gs, eo, em, ef, o_in, m_in, l_in,
    out_ref, w_ref, near_ref, far_ref, delta_ref, o_run, m_run, l_run, s_ref,
):
    _, late, _, _ = place(half, blk_count, span_ref)
    rows = out_ref.shape[0]
    big = qs.shape[0]
    pair = 2 * rows

    @pl.when(late)
    def _():
        def finish(cols, summed, total):
            alpha = jnp.exp2(m_in[:, cols] - m_run[:, cols])
            o_run[:, cols] = o_in[:, cols] * alpha + summed
            l_run[:, cols] = l_in[:, cols] * alpha + total

        attend_group((eo, em, ef), (None,) * 3, None, qs, m_in, m_run, w_ref, s_ref, finish)

    @pl.when(jnp.logical_not(late))
    def _():
        o_run[...] = o_in[...]
        m_run[...] = m_in[...]
        l_run[...] = l_in[...]

    ones = jnp.ones((8, HEAD), BF16)
    for p in range(big // pair):
        cols = slice(p * pair, (p + 1) * pair)
        inv = 1.0 / l_run[:, cols]
        far_ref[:, cols] = inv
        near_ref[:, cols] = inv * jnp.exp2(m_in[:, cols] - m_run[:, cols])
        o16 = (o_run[:, cols] * inv).astype(BF16).T
        out_ref[:, 2 * p * HEAD : (2 * p + 1) * HEAD] = o16[:rows]
        out_ref[:, (2 * p + 1) * HEAD : (2 * p + 2) * HEAD] = o16[rows:]
        prod = o16.astype(F32) * gs[cols, :].astype(F32)
        high = prod.astype(BF16)
        low = (prod - high.astype(F32)).astype(BF16)
        delta_ref[:, cols] = (dot_nt(ones, high) + dot_nt(ones, low))[:1]


def backward_unit(qs, gs, w_ref, slot, scale_ref, delta_ref, kv, gkv, gq_run, first, p_ref, d_ref):
    keys = kv.shape[0]
    big = qs.shape[0]
    pair = min(big, 2 * HEAD)
    kt = kv[:, :HEAD].T
    for c in range(0, big, pair):
        cols = slice(c, c + pair)
        prob = w_ref[slot * keys : (slot + 1) * keys, cols].astype(F32) * scale_ref[:, cols]
        dp = dot_nt(kv[:, HEAD:], gs[cols, :])
        p_ref[:, cols] = prob.astype(BF16)
        d_ref[:, cols] = (prob * (dp - delta_ref[:, cols])).astype(BF16)
    gkv[:, :HEAD] = (dot(d_ref[...], qs[...]) * FACTOR).astype(BF16)
    gkv[:, HEAD:] = dot(p_ref[...], gs[...]).astype(BF16)
    gq_run[...] = first[...] + dot(kt, d_ref[...])


def back_kernel(half, blk_count, which, span_ref, qs, gs, nw, fw, near_ref, far_ref, delta_ref, s_kv, e_kv, *refs):
    _, late, see_m, see_f = place(half, blk_count, span_ref)
    if which == "off":
        gs_out, ge_out, gq_run, ps, ds, pe, de = refs
        slot, see = 2, see_f
        gq_run[...] = jnp.zeros_like(gq_run)
        first = gq_run
    elif which == "mate":
        first, gs_out, ge_out, gq_run, ps, ds, pe, de = refs
        slot, see = 1, see_m
    else:
        first, gs_out, ge_out, gq_ref, gq_run, ps, ds, pe, de = refs
        slot, see = 0, None
    if which == "mate":

        @pl.when(jnp.logical_not(see))
        def _():
            gq_run[...] = first[...]

    visit(
        see,
        functools.partial(
            backward_unit, qs, gs, nw, slot, near_ref, delta_ref, s_kv, gs_out, gq_run, first, ps, ds
        ),
    )
    visit(
        late,
        functools.partial(
            backward_unit, qs, gs, fw, slot, far_ref, delta_ref, e_kv, ge_out, gq_run, gq_run, pe, de
        ),
    )
    for gkv, shown in ((gs_out, see), (ge_out, late)):
        if shown is not None:

            @pl.when(jnp.logical_not(shown))
            def _(gkv=gkv):
                gkv[...] = jnp.zeros_like(gkv)

    if which == "own":
        rows = gq_ref.shape[0]
        for h in range(qs.shape[0] // rows):
            g16 = (gq_run[:, h * rows : (h + 1) * rows] * FACTOR).astype(BF16)
            gq_ref[:, h * HEAD : (h + 1) * HEAD] = g16.T


def like(shape, dtype):
    return jax.ShapeDtypeStruct(shape, dtype)


def call(kernel, outs, scratch, units, args):
    rows, width = args[1].shape
    keys = sum(u.shape[0] for u in units)
    work = 2 * keys * rows * width
    return pl.pallas_call(
        kernel,
        out_shape=outs,
        in_specs=[SMEM] + [VMEM] * (len(args) - 1),
        out_specs=[VMEM] * len(outs),
        scratch_shapes=scratch,
        cost_estimate=pl.CostEstimate(flops=4 * work, bytes_accessed=4 * rows * width, transcendentals=work // 256),
        compiler_params=pltpu.CompilerParams(vmem_limit_bytes=30 << 20),
    )(*args)


def step(queries, key_rows, values, out_grad, span_order):
    rows, width = queries.shape
    grp_count = lax.axis_size("grp")
    blk_count = lax.axis_size("blk")
    half = grp_count // 2
    unit = half * rows
    big = width // HEAD * rows
    wide, line = like((HEAD, big), F32), like((1, big), F32)
    tile = like((unit, 2 * HEAD), BF16)
    full = like((rows, width), BF16)
    wide_s, line_s = pltpu.VMEM((HEAD, big), F32), pltpu.VMEM((1, big), F32)

    def send(block, grp_to, blk_to):
        route = []
        for g in range(grp_count):
            for b in range(blk_count):
                to = grp_to(g)
                if to is not None:
                    route.append((g * blk_count + b, to * blk_count + blk_to(b) % blk_count))
        return lax.ppermute(block, ("grp", "blk"), route)

    same = lambda i: i
    on_chip = lambda block: send(block, same, lambda b: b ^ 1)
    off_chip = lambda block: send(block, same, lambda b: b + 1 if b % 2 else b - 1)
    ring_up = lambda block: send(block, lambda g: g // half * half + (g + 1) % half, same)
    ring_down = lambda block: send(block, lambda g: g // half * half + (g - 1) % half, same)
    to_late = lambda block: send(block, lambda g: g + half if g < half else None, same)
    to_early = lambda block: send(block, lambda g: g - half if g >= half else None, same)

    def gathered(block):
        parts = [block]
        for _ in range(half - 1):
            parts.append(ring_up(parts[-1]))
        return jnp.concatenate(parts, axis=0)

    def scattered(block):
        slots = [block[s * rows : (s + 1) * rows] for s in range(half)]
        total = slots[-1]
        for s in range(half - 2, -1, -1):
            moved = ring_down(total)
            total = add(moved, slots[s])
        return total

    add = lambda a, b: (a.astype(F32) + b.astype(F32)).astype(BF16)
    own = lax.optimization_barrier(jnp.concatenate([key_rows, values], axis=1))
    off = off_chip(own)
    so = gathered(own)
    sf = gathered(off)
    sm = on_chip(so)
    eo = to_late(so)
    ef = to_late(sf)
    em = on_chip(eo)

    stack = like((big, HEAD), BF16)
    weights = like((3 * unit, big), BF16)
    scores = pltpu.VMEM((3, unit, big), F32)
    o_run, m_run, l_run, nw, qs, gs = call(
        functools.partial(near_kernel, half, blk_count), [wide, line, line, weights, stack, stack], [scores],
        [so, sm, sf], [span_order, queries, out_grad, so, sm, sf],
    )
    out, fw, near, far, delta = call(
        functools.partial(far_kernel, half, blk_count), [full, weights, line, line, line],
        [wide_s, line_s, line_s, scores],
        [eo, em, ef], [span_order, qs, gs, eo, em, ef, o_run, m_run, l_run],
    )

    state = [span_order, qs, gs, nw, fw, near, far, delta]
    back = lambda which: functools.partial(back_kernel, half, blk_count, which)
    temp = [pltpu.VMEM((unit, big), BF16)] * 4
    gsf, gef, gq = call(back("off"), [tile, tile, wide], temp, [sf, ef], state + [sf, ef])
    gsm, gem, gq = call(back("mate"), [tile, tile, wide], temp, [sm, em], state + [sm, em, gq])
    gso, geo, gq = call(back("own"), [tile, tile, full], [wide_s] + temp, [so, eo], state + [so, eo, gq])

    back_f = to_early(gef)
    gsf = add(gsf, back_f)
    total_f = scattered(gsf)
    ret_f = off_chip(total_f)
    mate = on_chip(jnp.concatenate([gsm, gem], axis=0))
    geo = add(geo, mate[unit:])
    back_o = to_early(geo)
    gso = gso.astype(F32) + mate[:unit].astype(F32)
    gso = (gso + back_o.astype(F32)).astype(BF16)
    final = add(scattered(gso), ret_f)
    return (out, gq, final[:, :HEAD], final[:, HEAD:])


def solution(mesh):
    spec = P(("grp", "blk"), None)
    return jax.shard_map(
        step,
        mesh=mesh,
        in_specs=(spec, spec, spec, spec, P()),
        out_specs=(spec, spec, spec, spec),
        check_vma=False,
    )
```

```python
import functools
import math

import jax
import jax.numpy as jnp
from jax import lax
from jax.experimental import pallas as pl
from jax.experimental.pallas import tpu as pltpu
from jax.sharding import PartitionSpec as P


HEAD = 128
NEG_FILL = -1e30
F32 = jnp.float32
BF16 = jnp.bfloat16
NT = (((1,), (1,)), ((), ()))
FACTOR = 1.0 / math.sqrt(HEAD)
C2 = FACTOR * math.log2(math.e)
VMEM = pl.BlockSpec(memory_space=pltpu.VMEM)


def dot(a, b):
    return jnp.dot(a, b, preferred_element_type=F32)


def dot_nt(a, b):
    return lax.dot_general(a, b, NT, preferred_element_type=F32)


def biases(half, blk_count, span_ref):
    blk = lax.axis_index("blk")
    late = lax.axis_index("grp") >= half
    step = jnp.where(lax.rem(blk, 2) == 0, 1, -1)
    span = span_ref[...]
    ids = lax.broadcasted_iota(jnp.int32, span.shape, 1)
    pick = lambda b: jnp.sum(jnp.where(ids == lax.rem(b + blk_count, blk_count), span, 0), axis=1, keepdims=True)
    mine = pick(blk)
    sign = jnp.where(late, 1, -1)
    hidden = lambda other: jnp.where((pick(other) - mine) * sign > 0, 0.0, NEG_FILL)
    return hidden(blk + step), hidden(blk - step)


def is_late(half):
    return lax.axis_index("grp") >= half


def own_mask(keys, rows, idx):
    row = lax.broadcasted_iota(jnp.int32, (keys, 2 * rows), 0)
    col = lax.broadcasted_iota(jnp.int32, (keys, 2 * rows), 1)
    col = jnp.where(col >= rows, col - rows, col)
    return (row <= col) | ((row >= rows) & (row < (idx + 1) * rows))


def attend_group(units, bias, mask, qs, m_in, m_ref, w_ref, s_ref, finish):
    keys = units[0].shape[0]
    big = qs.shape[0]
    pair = min(big, 2 * HEAD)
    ones = jnp.ones((16, keys), BF16)
    for c in range(0, big, pair):
        cols = slice(c, c + pair)
        top = m_in[:, cols] if m_in is not None else jnp.full((1, pair), NEG_FILL, F32)
        for u, kv in enumerate(units):
            s = dot_nt(kv[:, :HEAD], qs[cols, :]) * C2
            if u == 0 and mask is not None:
                s = jnp.where(mask, s, NEG_FILL)
            s_ref[u, :, cols] = s
            peak = jnp.max(s, axis=0, keepdims=True)
            if u > 0 and bias is not None:
                peak = jnp.where(bias[u - 1] < 0.0, NEG_FILL, peak)
            top = jnp.maximum(top, peak)
        m_ref[:, cols] = top
    vt = jnp.concatenate([jnp.concatenate([kv[:, HEAD:].T, ones], axis=0) for kv in units], axis=1)
    for c in range(0, big, pair):
        cols = slice(c, c + pair)
        for u in range(len(units)):
            base = m_ref[:, cols]
            if u > 0 and bias is not None:
                base = jnp.where(bias[u - 1] < 0.0, -NEG_FILL, base)
            w_ref[u * keys : (u + 1) * keys, cols] = jnp.exp2(s_ref[u, :, cols] - base).astype(BF16)
        summed = dot(vt, w_ref[:, cols])
        finish(cols, summed[:HEAD], summed[HEAD : HEAD + 1])


def near_kernel(rows, half, blk_count, span_ref, qs, so, sm, sf, o_ref, m_ref, l_ref, w_ref, s_ref):
    idx = lax.rem(lax.axis_index("grp"), half)

    def finish(cols, summed, total):
        o_ref[:, cols] = summed
        l_ref[:, cols] = total

    mask = own_mask(so.shape[0], rows, idx)
    bias = biases(half, blk_count, span_ref)
    attend_group((so, sm, sf), bias, mask, qs, None, m_ref, w_ref, s_ref, finish)


def far_kernel(
    half, qs, gs, eo, em, ef, o_in, m_in, l_in,
    out_ref, w_ref, near_ref, far_ref, delta_ref, o_run, m_run, l_run, s_ref,
):
    late = is_late(half)
    rows = out_ref.shape[0]
    big = qs.shape[0]
    pair = 2 * rows

    @pl.when(late)
    def _():
        def finish(cols, summed, total):
            alpha = jnp.exp2(m_in[:, cols] - m_run[:, cols])
            o_run[:, cols] = o_in[:, cols] * alpha + summed
            l_run[:, cols] = l_in[:, cols] * alpha + total

        attend_group((eo, em, ef), None, None, qs, m_in, m_run, w_ref, s_ref, finish)

    @pl.when(jnp.logical_not(late))
    def _():
        o_run[...] = o_in[...]
        m_run[...] = m_in[...]
        l_run[...] = l_in[...]

    ones = jnp.ones((8, HEAD), BF16)
    for p in range(big // pair):
        cols = slice(p * pair, (p + 1) * pair)
        inv = 1.0 / l_run[:, cols]
        far_ref[:, cols] = inv
        near_ref[:, cols] = inv * jnp.exp2(m_in[:, cols] - m_run[:, cols])
        o16 = (o_run[:, cols] * inv).astype(BF16).T
        out_ref[:, 2 * p * HEAD : (2 * p + 1) * HEAD] = o16[:rows]
        out_ref[:, (2 * p + 1) * HEAD : (2 * p + 2) * HEAD] = o16[rows:]
        prod = o16.astype(F32) * gs[cols, :].astype(F32)
        high = prod.astype(BF16)
        low = (prod - high.astype(F32)).astype(BF16)
        delta_ref[:, cols] = (dot_nt(ones, high) + dot_nt(ones, low))[:1]


def backward_unit(qs, gs, w_ref, slot, scale_ref, delta_ref, kv, gkv, gq_run, first, p_ref, d_ref):
    keys = kv.shape[0]
    big = qs.shape[0]
    pair = min(big, 2 * HEAD)
    kt = kv[:, :HEAD].T
    for c in range(0, big, pair):
        cols = slice(c, c + pair)
        prob = w_ref[slot * keys : (slot + 1) * keys, cols].astype(F32) * scale_ref[:, cols]
        dp = dot_nt(kv[:, HEAD:], gs[cols, :])
        p_ref[:, cols] = prob.astype(BF16)
        d_ref[:, cols] = (prob * (dp - delta_ref[:, cols])).astype(BF16)
    gkv[:, :HEAD] = (dot(d_ref[...], qs[...]) * FACTOR).astype(BF16)
    gkv[:, HEAD:] = dot(p_ref[...], gs[...]).astype(BF16)
    more = dot(kt, d_ref[...])
    gq_run[...] = more if first is None else first[...] + more


def back_kernel(half, parts, has_first, last, qs, gs, delta_ref, *refs):
    late = is_late(half)
    refs = list(refs)
    take = lambda n: [refs.pop(0) for _ in range(n)]
    ins = [take(3) for _ in parts]
    first = take(1)[0] if has_first else None
    outs = take(1 + max(p[2] for p in parts))
    gq_ref = take(1)[0] if last else None
    gq_run = take(1)[0]
    keys = ins[0][2].shape[0]
    for i, ((far, slot, out, row), (w_ref, scale_ref, kv)) in enumerate(zip(parts, ins)):
        gkv = outs[out].at[row * keys : (row + 1) * keys, :]
        p_ref, d_ref = refs[2 * i], refs[2 * i + 1]
        base = first if i == 0 else gq_run
        run = functools.partial(
            backward_unit, qs, gs, w_ref, slot, scale_ref, delta_ref, kv, gkv, gq_run, base, p_ref, d_ref
        )
        if far:
            pl.when(late)(run)

            @pl.when(jnp.logical_not(late))
            def _(gkv=gkv, base=base):
                gkv[...] = jnp.zeros_like(gkv)
                if base is not gq_run:
                    gq_run[...] = jnp.zeros_like(gq_run) if base is None else base[...]
        else:
            run()
    if last:
        rows = gq_ref.shape[0]
        for h in range(qs.shape[0] // rows):
            g16 = (gq_run[:, h * rows : (h + 1) * rows] * FACTOR).astype(BF16)
            gq_ref[:, h * HEAD : (h + 1) * HEAD] = g16.T


def like(shape, dtype):
    return jax.ShapeDtypeStruct(shape, dtype)


def call(kernel, outs, scratch, keys, args, spec=VMEM):
    work = 2 * keys * HEAD * HEAD * 8
    return pl.pallas_call(
        kernel,
        out_shape=outs,
        in_specs=[spec] * len(args),
        out_specs=[VMEM] * len(outs),
        scratch_shapes=scratch,
        cost_estimate=pl.CostEstimate(flops=4 * work, bytes_accessed=1 << 20, transcendentals=work // 256),
        compiler_params=pltpu.CompilerParams(vmem_limit_bytes=30 << 20),
    )(*args)


def step(queries, key_rows, values, out_grad, span_order):
    rows, width = queries.shape
    grp_count = lax.axis_size("grp")
    blk_count = lax.axis_size("blk")
    half = grp_count // 2
    unit = half * rows
    big = width // HEAD * rows
    wide, line = like((HEAD, big), F32), like((1, big), F32)
    full = like((rows, width), BF16)
    wide_s, line_s = pltpu.VMEM((HEAD, big), F32), pltpu.VMEM((1, big), F32)

    def send(block, grp_to, blk_to):
        route = []
        for g in range(grp_count):
            for b in range(blk_count):
                to = grp_to(g)
                if to is not None:
                    route.append((g * blk_count + b, to * blk_count + blk_to(b) % blk_count))
        return lax.ppermute(block, ("grp", "blk"), route)

    same = lambda i: i
    on_chip = lambda block: send(block, same, lambda b: b ^ 1)
    off_chip = lambda block: send(block, same, lambda b: b + 1 if b % 2 else b - 1)
    ring_up = lambda block: send(block, lambda g: g // half * half + (g + 1) % half, same)
    ring_down = lambda block: send(block, lambda g: g // half * half + (g - 1) % half, same)
    across = lambda block: send(block, lambda g: (g + half) % grp_count, same)

    def gathered(block):
        parts = [block]
        for _ in range(half - 1):
            parts.append(ring_up(parts[-1]))
        return jnp.concatenate(parts, axis=0)

    def scattered(block):
        slots = [block[s * rows : (s + 1) * rows] for s in range(half)]
        total = slots[-1]
        for s in range(half - 2, -1, -1):
            moved = ring_down(total)
            total = add(moved, slots[s])
        return total

    add = lambda a, b: (a.astype(F32) + b.astype(F32)).astype(BF16)
    own = lax.optimization_barrier(jnp.concatenate([key_rows, values], axis=1))

    def stacked(x):
        x = jnp.transpose(x.reshape(rows, width // HEAD, HEAD), (1, 0, 2))
        return lax.optimization_barrier(x.reshape(big, HEAD))

    qs, gs = stacked(queries), stacked(out_grad)

    off = off_chip(own)
    so = gathered(own)
    sf = gathered(off)
    sm = on_chip(so)
    eo = across(so)
    ef = across(sf)
    em = on_chip(eo)

    weights = like((3 * unit, big), BF16)
    scores = pltpu.VMEM((3, unit, big), F32)
    o_run, m_run, l_run, nw = call(
        functools.partial(near_kernel, rows, half, blk_count), [wide, line, line, weights], [scores],
        3 * unit, [span_order.reshape(1, blk_count), qs, so, sm, sf],
    )
    out, fw, near, far, delta = call(
        functools.partial(far_kernel, half), [full, weights, line, line, line], [wide_s, line_s, line_s, scores],
        3 * unit, [qs, gs, eo, em, ef, o_run, m_run, l_run],
    )

    def back(parts, first, last=False):
        args = [qs, gs, delta]
        for far_part, slot, out_index, row, kv in parts:
            args += [fw, far, kv] if far_part else [nw, near, kv]
        if first is not None:
            args.append(first)
        shape = tuple(p[:4] for p in parts)
        sizes = [sum(p[2] == i for p in shape) for i in range(1 + max(p[2] for p in shape))]
        outs = [like((n * unit, 2 * HEAD), BF16) for n in sizes] + [full if last else wide]
        temp = ([wide_s] if last else []) + [pltpu.VMEM((unit, big), BF16)] * (2 * len(parts))
        kernel = functools.partial(back_kernel, half, shape, first is not None, last)
        return call(kernel, outs, temp, unit * len(parts), args)

    gef, gq = back([(True, 2, 0, 0, ef)], None)
    gm, gq = back([(True, 1, 0, 1, em), (False, 1, 0, 0, sm)], gq)
    geo, gsf, gq = back([(True, 0, 0, 0, eo), (False, 2, 1, 0, sf)], gq)
    gso, gq = back([(False, 0, 0, 0, so)], gq, last=True)

    back_f = across(gef)
    gsf = add(gsf, back_f)
    total_f = scattered(gsf)
    ret_f = off_chip(total_f)
    mate = on_chip(gm)
    geo = add(geo, mate[unit:])
    back_o = across(geo)
    gso = gso.astype(F32) + mate[:unit].astype(F32)
    gso = (gso + back_o.astype(F32)).astype(BF16)
    final = add(scattered(gso), ret_f)
    return (out, gq, final[:, :HEAD], final[:, HEAD:])


def solution(mesh):
    spec = P(("grp", "blk"), None)
    return jax.shard_map(
        step,
        mesh=mesh,
        in_specs=(spec, spec, spec, spec, P()),
        out_specs=(spec, spec, spec, spec),
        check_vma=False,
    )
```

```python
import functools
import math

import jax
import jax.numpy as jnp
from jax import lax
from jax.experimental import pallas as pl
from jax.experimental.pallas import tpu as pltpu
from jax.sharding import PartitionSpec as P


HEAD = 128
NEG_FILL = -1e30
F32 = jnp.float32
BF16 = jnp.bfloat16
NT = (((1,), (1,)), ((), ()))
FACTOR = 1.0 / math.sqrt(HEAD)
C2 = FACTOR * math.log2(math.e)
VMEM = pl.BlockSpec(memory_space=pltpu.VMEM)


def dot(a, b):
    return jnp.dot(a, b, preferred_element_type=F32)


def dot_nt(a, b):
    return lax.dot_general(a, b, NT, preferred_element_type=F32)


def biases(half, blk_count, span_ref):
    blk = lax.axis_index("blk")
    late = lax.axis_index("grp") >= half
    step = jnp.where(lax.rem(blk, 2) == 0, 1, -1)
    span = span_ref[...]
    ids = lax.broadcasted_iota(jnp.int32, span.shape, 1)
    pick = lambda b: jnp.sum(jnp.where(ids == lax.rem(b + blk_count, blk_count), span, 0), axis=1, keepdims=True)
    mine = pick(blk)
    sign = jnp.where(late, 1, -1)
    hidden = lambda other: jnp.where((pick(other) - mine) * sign > 0, 0.0, NEG_FILL)
    return hidden(blk + step), hidden(blk - step)


def is_late(half):
    return lax.axis_index("grp") >= half


def own_mask(keys, rows, idx):
    row = lax.broadcasted_iota(jnp.int32, (keys, 2 * rows), 0)
    col = lax.broadcasted_iota(jnp.int32, (keys, 2 * rows), 1)
    col = jnp.where(col >= rows, col - rows, col)
    return (row <= col) | ((row >= rows) & (row < (idx + 1) * rows))


def attend_group(units, bias, mask, qs, m_in, m_ref, w_ref, s_ref, finish):
    keys = units[0].shape[0]
    big = qs.shape[0]
    pair = min(big, 2 * HEAD)
    ones = jnp.ones((16, keys), BF16)
    for c in range(0, big, pair):
        cols = slice(c, c + pair)
        top = m_in[:, cols] if m_in is not None else jnp.full((1, pair), NEG_FILL, F32)
        for u, kv in enumerate(units):
            s = dot_nt(kv[:, :HEAD], qs[cols, :]) * C2
            if u == 0 and mask is not None:
                s = jnp.where(mask, s, NEG_FILL)
            s_ref[u, :, cols] = s
            peak = jnp.max(s, axis=0, keepdims=True)
            if u > 0 and bias is not None:
                peak = jnp.where(bias[u - 1] < 0.0, NEG_FILL, peak)
            top = jnp.maximum(top, peak)
        m_ref[:, cols] = top
    vt = jnp.concatenate([jnp.concatenate([kv[:, HEAD:].T, ones], axis=0) for kv in units], axis=1)
    for c in range(0, big, pair):
        cols = slice(c, c + pair)
        for u in range(len(units)):
            base = m_ref[:, cols]
            if u > 0 and bias is not None:
                base = jnp.where(bias[u - 1] < 0.0, -NEG_FILL, base)
            w_ref[u * keys : (u + 1) * keys, cols] = jnp.exp2(s_ref[u, :, cols] - base).astype(BF16)
        summed = dot(vt, w_ref[:, cols])
        finish(cols, summed[:HEAD], summed[HEAD : HEAD + 1])


def near_kernel(rows, half, blk_count, span_ref, qs, so, sm, sf, o_ref, m_ref, l_ref, w_ref, s_ref):
    idx = lax.rem(lax.axis_index("grp"), half)

    def finish(cols, summed, total):
        o_ref[:, cols] = summed
        l_ref[:, cols] = total

    mask = own_mask(so.shape[0], rows, idx)
    bias = biases(half, blk_count, span_ref)
    attend_group((so, sm, sf), bias, mask, qs, None, m_ref, w_ref, s_ref, finish)


def far_kernel(
    half, qs, gs, eo, em, ef, o_in, m_in, l_in,
    out_ref, w_ref, near_ref, far_ref, delta_ref, o_run, m_run, l_run, s_ref,
):
    late = is_late(half)
    rows = out_ref.shape[0]
    big = qs.shape[0]
    pair = 2 * rows

    @pl.when(late)
    def _():
        def finish(cols, summed, total):
            alpha = jnp.exp2(m_in[:, cols] - m_run[:, cols])
            o_run[:, cols] = o_in[:, cols] * alpha + summed
            l_run[:, cols] = l_in[:, cols] * alpha + total

        attend_group((eo, em, ef), None, None, qs, m_in, m_run, w_ref, s_ref, finish)

    @pl.when(jnp.logical_not(late))
    def _():
        o_run[...] = o_in[...]
        m_run[...] = m_in[...]
        l_run[...] = l_in[...]

    ones = jnp.ones((8, HEAD), BF16)
    for p in range(big // pair):
        cols = slice(p * pair, (p + 1) * pair)
        inv = 1.0 / l_run[:, cols]
        far_ref[:, cols] = inv
        near_ref[:, cols] = inv * jnp.exp2(m_in[:, cols] - m_run[:, cols])
        o16 = (o_run[:, cols] * inv).astype(BF16).T
        out_ref[:, 2 * p * HEAD : (2 * p + 1) * HEAD] = o16[:rows]
        out_ref[:, (2 * p + 1) * HEAD : (2 * p + 2) * HEAD] = o16[rows:]
        prod = o16.astype(F32) * gs[cols, :].astype(F32)
        high = prod.astype(BF16)
        low = (prod - high.astype(F32)).astype(BF16)
        delta_ref[:, cols] = (dot_nt(ones, high) + dot_nt(ones, low))[:1]


def backward_unit(qs, gs, w_ref, slot, scale_ref, delta_ref, kv, gkv, gq_run, first, p_ref, d_ref):
    keys = kv.shape[0]
    big = qs.shape[0]
    pair = min(big, 2 * HEAD)
    kt = kv[:, :HEAD].T
    for c in range(0, big, pair):
        cols = slice(c, c + pair)
        prob = w_ref[slot * keys : (slot + 1) * keys, cols].astype(F32) * scale_ref[:, cols]
        dp = dot_nt(kv[:, HEAD:], gs[cols, :])
        p_ref[:, cols] = prob.astype(BF16)
        d_ref[:, cols] = (prob * (dp - delta_ref[:, cols])).astype(BF16)
    gkv[:, :HEAD] = (dot(d_ref[...], qs[...]) * FACTOR).astype(BF16)
    gkv[:, HEAD:] = dot(p_ref[...], gs[...]).astype(BF16)
    more = dot(kt, d_ref[...])
    gq_run[...] = more if first is None else first[...] + more


def back_kernel(half, parts, blanks, carried, new, last, qs, gs, delta_ref, *refs):
    late = is_late(half)
    refs = list(refs)
    take = lambda n: [refs.pop(0) for _ in range(n)]
    ins = [take(3) for _ in parts]
    kept = take(1)[0] if last else None
    first = take(carried)[-1] if carried else None
    outs = take(new)
    gq_ref, out_ref = take(2) if last else (None, None)
    gq_run = take(1)[0]
    if last:
        copy = pltpu.make_async_copy(kept, out_ref, refs.pop())
        copy.start()
    keys = ins[0][2].shape[0]
    block = lambda out, row: outs[out].at[row * keys : (row + 1) * keys, :]
    for when in ("late", "early", "all"):
        chosen = [i for i, p in enumerate(parts) if p[0] == when]
        empty = [block(out, row) for w, out, row in blanks if w == when]
        if not chosen and not empty:
            continue

        def run(chosen=chosen, empty=empty):
            for ref in empty:
                ref[...] = jnp.zeros_like(ref)
            for n, i in enumerate(chosen):
                _, slot, out, row = parts[i][1:]
                w_ref, scale_ref, kv = ins[i]
                backward_unit(
                    qs, gs, w_ref, slot, scale_ref, delta_ref, kv, block(out, row), gq_run,
                    first if n == 0 else gq_run, refs[2 * n], refs[2 * n + 1],
                )

        if when == "all":
            run()
        else:
            pl.when(late if when == "late" else jnp.logical_not(late))(run)
    if last:
        rows = gq_ref.shape[0]
        for h in range(qs.shape[0] // rows):
            g16 = (gq_run[:, h * rows : (h + 1) * rows] * FACTOR).astype(BF16)
            gq_ref[:, h * HEAD : (h + 1) * HEAD] = g16.T
        copy.wait()


def like(shape, dtype):
    return jax.ShapeDtypeStruct(shape, dtype)


def call(kernel, outs, scratch, keys, args, out_specs=None, aliases={}):
    work = 2 * keys * HEAD * HEAD * 8
    return pl.pallas_call(
        kernel,
        out_shape=outs,
        in_specs=[VMEM] * len(args),
        out_specs=out_specs or [VMEM] * len(outs),
        scratch_shapes=scratch,
        input_output_aliases=aliases,
        cost_estimate=pl.CostEstimate(flops=4 * work, bytes_accessed=1 << 20, transcendentals=work // 256),
        compiler_params=pltpu.CompilerParams(vmem_limit_bytes=30 << 20),
    )(*args)


def step(queries, key_rows, values, out_grad, span_order):
    rows, width = queries.shape
    grp_count = lax.axis_size("grp")
    blk_count = lax.axis_size("blk")
    half = grp_count // 2
    unit = half * rows
    big = width // HEAD * rows
    wide, line = like((HEAD, big), F32), like((1, big), F32)
    full = like((rows, width), BF16)
    wide_s, line_s = pltpu.VMEM((HEAD, big), F32), pltpu.VMEM((1, big), F32)

    def send(block, grp_to, blk_to):
        route = []
        for g in range(grp_count):
            for b in range(blk_count):
                to = grp_to(g)
                if to is not None:
                    route.append((g * blk_count + b, to * blk_count + blk_to(b) % blk_count))
        return lax.ppermute(block, ("grp", "blk"), route)

    same = lambda i: i
    on_chip = lambda block: send(block, same, lambda b: b ^ 1)
    off_chip = lambda block: send(block, same, lambda b: b + 1 if b % 2 else b - 1)
    ring_up = lambda block: send(block, lambda g: g // half * half + (g + 1) % half, same)
    ring_down = lambda block: send(block, lambda g: g // half * half + (g - 1) % half, same)
    across = lambda block: send(block, lambda g: (g + half) % grp_count, same)

    def gathered(block):
        parts = [block]
        for _ in range(half - 1):
            parts.append(ring_up(parts[-1]))
        return jnp.concatenate(parts, axis=0)

    def scattered(block):
        slots = [block[s * rows : (s + 1) * rows] for s in range(half)]
        total = slots[-1]
        for s in range(half - 2, -1, -1):
            moved = ring_down(total)
            total = add(moved, slots[s])
        return total

    add = lambda a, b: (a.astype(F32) + b.astype(F32)).astype(BF16)
    own = lax.optimization_barrier(jnp.concatenate([key_rows, values], axis=1))

    def stacked(x):
        x = jnp.transpose(x.reshape(rows, width // HEAD, HEAD), (1, 0, 2))
        return lax.optimization_barrier(x.reshape(big, HEAD))

    qs, gs = stacked(queries), stacked(out_grad)

    off = off_chip(own)
    so = gathered(own)
    sf = gathered(off)
    sm = on_chip(so)
    eo = across(so)
    ef = across(sf)
    em = on_chip(eo)

    weights = like((3 * unit, big), BF16)
    scores = pltpu.VMEM((3, unit, big), F32)
    o_run, m_run, l_run, nw = call(
        functools.partial(near_kernel, rows, half, blk_count), [wide, line, line, weights], [scores],
        3 * unit, [span_order.reshape(1, blk_count), qs, so, sm, sf],
    )
    kept, fw, near, far, delta = call(
        functools.partial(far_kernel, half), [full, weights, line, line, line], [wide_s, line_s, line_s, scores],
        3 * unit, [qs, gs, eo, em, ef, o_run, m_run, l_run],
    )

    def back(parts, blanks, carry, sizes, gq, last=False):
        args = [qs, gs, delta]
        for _, far_part, slot, _, _, kv in parts:
            args += [fw, far, kv] if far_part else [nw, near, kv]
        if last:
            args.append(kept)
        carried = list(carry) + ([] if gq is None else [gq])
        base = len(args)
        args += carried
        outs = [like(a.shape, a.dtype) for a in carry] + [like((n, 2 * HEAD), BF16) for n in sizes]
        aliases = {base + i: i for i in range(len(carry))}
        new = len(outs)
        temp = [pltpu.VMEM((unit, big), BF16)] * (2 * len(parts))
        specs = None
        if last:
            outs += [full, full]
            specs = [VMEM] * (len(outs) - 1) + [pl.BlockSpec(memory_space=pl.ANY)]
            temp = [wide_s] + temp + [pltpu.SemaphoreType.DMA]
        else:
            outs.append(wide)
            if gq is not None:
                aliases[base + len(carry)] = len(outs) - 1
        shape = tuple(p[:5] for p in parts)
        kernel = functools.partial(back_kernel, half, shape, blanks, len(carried), new, last)
        return call(kernel, outs, temp, unit * len(parts), args, specs, aliases)

    gef, gsf, gm, gq = back(
        [("late", True, 2, 0, 0, ef), ("early", False, 2, 1, 0, sf), ("early", False, 1, 2, 0, sm)],
        (("early", 0, 0), ("early", 2, 1)), [], [unit, unit, 2 * unit], None,
    )
    gm, gq = back([("late", True, 1, 0, 1, em), ("late", False, 1, 0, 0, sm)], (), [gm], [], gq)
    gsf, geo, gq = back(
        [("late", True, 0, 1, 0, eo), ("late", False, 2, 0, 0, sf)], (("early", 1, 0),), [gsf], [unit], gq
    )
    gso, gq, out = back([("all", False, 0, 0, 0, so)], (), [], [unit], gq, last=True)

    back_f = across(gef)
    gsf = add(gsf, back_f)
    total_f = scattered(gsf)
    ret_f = off_chip(total_f)
    mate = on_chip(gm)
    geo = add(geo, mate[unit:])
    back_o = across(geo)
    gso = gso.astype(F32) + mate[:unit].astype(F32)
    gso = (gso + back_o.astype(F32)).astype(BF16)
    final = add(scattered(gso), ret_f)
    return (out, gq, final[:, :HEAD], final[:, HEAD:])


def solution(mesh):
    spec = P(("grp", "blk"), None)
    return jax.shard_map(
        step,
        mesh=mesh,
        in_specs=(spec, spec, spec, spec, P()),
        out_specs=(spec, spec, spec, spec),
        check_vma=False,
    )
```

```python
import functools
import math

import jax
import jax.numpy as jnp
from jax import lax
from jax.experimental import pallas as pl
from jax.experimental.pallas import tpu as pltpu
from jax.sharding import PartitionSpec as P


HEAD = 128
NEG_FILL = -1e30
F32 = jnp.float32
BF16 = jnp.bfloat16
NT = (((1,), (1,)), ((), ()))
FACTOR = 1.0 / math.sqrt(HEAD)
C2 = FACTOR * math.log2(math.e)
VMEM = pl.BlockSpec(memory_space=pltpu.VMEM)


def dot(a, b):
    return jnp.dot(a, b, preferred_element_type=F32)


def dot_nt(a, b):
    return lax.dot_general(a, b, NT, preferred_element_type=F32)


def biases(half, blk_count, span_ref):
    blk = lax.axis_index("blk")
    late = lax.axis_index("grp") >= half
    step = jnp.where(lax.rem(blk, 2) == 0, 1, -1)
    span = span_ref[...]
    ids = lax.broadcasted_iota(jnp.int32, span.shape, 1)
    pick = lambda b: jnp.sum(jnp.where(ids == lax.rem(b + blk_count, blk_count), span, 0), axis=1, keepdims=True)
    mine = pick(blk)
    sign = jnp.where(late, 1, -1)
    hidden = lambda other: jnp.where((pick(other) - mine) * sign > 0, 0.0, NEG_FILL)
    return hidden(blk + step), hidden(blk - step)


def is_late(half):
    return lax.axis_index("grp") >= half


def own_mask(keys, rows, idx):
    row = lax.broadcasted_iota(jnp.int32, (keys, 2 * rows), 0)
    col = lax.broadcasted_iota(jnp.int32, (keys, 2 * rows), 1)
    col = jnp.where(col >= rows, col - rows, col)
    return (row <= col) | ((row >= rows) & (row < (idx + 1) * rows))


def load(refs, rows, far, column):
    tiles = []
    for ref in refs:
        for r in range(far * rows, ref.shape[0], 2 * rows):
            tiles.append(ref[r : r + rows, column : column + HEAD])
    return jnp.concatenate(tiles, axis=0) if len(tiles) > 1 else tiles[0]


def attend_group(refs, rows, count, hidden, mask, qs, m_in, m_ref, w_ref, s_ref, finish):
    big = qs.shape[0]
    pair = min(big, 2 * HEAD)
    ks = [load(refs, rows, u, 0) for u in range(count)]
    keys = ks[0].shape[0]
    ones = jnp.ones((16, keys), BF16)
    for c in range(0, big, pair):
        cols = slice(c, c + pair)
        top = m_in[:, cols] if m_in is not None else jnp.full((1, pair), NEG_FILL, F32)
        for u, k in enumerate(ks):
            s = dot_nt(k, qs[cols, :]) * C2
            if u == 0 and mask is not None:
                s = jnp.where(mask, s, NEG_FILL)
            s_ref[u, :, cols] = s
            peak = jnp.max(s, axis=0, keepdims=True)
            if u == 0 and hidden is not None:
                peak = jnp.where(hidden < 0.0, NEG_FILL, peak)
            top = jnp.maximum(top, peak)
        m_ref[:, cols] = top
    vt = [jnp.concatenate([load(refs, rows, u, HEAD).T, ones], axis=0) for u in range(count)]
    vt = jnp.concatenate(vt, axis=1) if count > 1 else vt[0]
    for c in range(0, big, pair):
        cols = slice(c, c + pair)
        for u in range(count):
            base = m_ref[:, cols]
            if u == 0 and hidden is not None:
                base = jnp.where(hidden < 0.0, -NEG_FILL, base)
            w_ref[u * keys : (u + 1) * keys, cols] = jnp.exp2(s_ref[u, :, cols] - base).astype(BF16)
        summed = dot(vt, w_ref[: count * keys, cols])
        finish(cols, summed[:HEAD], summed[HEAD : HEAD + 1])


def attend_block(which, rows, half, blk_count, span_ref, qs, refs, before, o_run, m_run, l_run, w_ref, s_ref):
    late = is_late(half)
    o_in, m_in, l_in = before or (None, None, None)

    def finish(cols, summed, total):
        if before:
            alpha = jnp.exp2(m_in[:, cols] - m_run[:, cols])
            summed = o_in[:, cols] * alpha + summed
            total = l_in[:, cols] * alpha + total
        o_run[:, cols] = summed
        l_run[:, cols] = total

    hidden = mask = None
    if which == 0:
        mask = own_mask(half * rows, rows, lax.rem(lax.axis_index("grp"), half))
    else:
        hidden = biases(half, blk_count, span_ref)[which - 1]
    for count, on in ((2, late), (1, jnp.logical_not(late))):
        pl.when(on)(
            functools.partial(attend_group, refs, rows, count, hidden, mask, qs, m_in, m_run, w_ref, s_ref, finish)
        )


def forward_kernel(which, rows, half, blk_count, span_ref, qs, *refs):
    refs = list(refs)
    o_run, m_run, l_run, w_ref, s_ref = refs[-5:]
    before = refs[-8:-5] if which else None
    attend_block(
        which, rows, half, blk_count, span_ref, qs, refs[: -8 if which else -5], before, o_run, m_run, l_run, w_ref, s_ref
    )


def finish_kernel(rows, half, blk_count, span_ref, qs, gs, *refs):
    refs = list(refs)
    m_first, o_in, m_in, l_in, out_ref, w_ref, a_ref, b_ref, c_ref, delta_ref, o_run, m_run, l_run, s_ref = refs[-14:]
    attend_block(
        2, rows, half, blk_count, span_ref, qs, refs[:-14], (o_in, m_in, l_in), o_run, m_run, l_run, w_ref, s_ref
    )
    big = qs.shape[0]
    pair = 2 * rows
    ones = jnp.ones((8, HEAD), BF16)
    for p in range(big // pair):
        cols = slice(p * pair, (p + 1) * pair)
        inv = 1.0 / l_run[:, cols]
        a_ref[:, cols] = inv * jnp.exp2(m_first[:, cols] - m_run[:, cols])
        b_ref[:, cols] = inv * jnp.exp2(m_in[:, cols] - m_run[:, cols])
        c_ref[:, cols] = inv
        o16 = (o_run[:, cols] * inv).astype(BF16).T
        out_ref[:, 2 * p * HEAD : (2 * p + 1) * HEAD] = o16[:rows]
        out_ref[:, (2 * p + 1) * HEAD : (2 * p + 2) * HEAD] = o16[rows:]
        prod = o16.astype(F32) * gs[cols, :].astype(F32)
        high = prod.astype(BF16)
        low = (prod - high.astype(F32)).astype(BF16)
        delta_ref[:, cols] = (dot_nt(ones, high) + dot_nt(ones, low))[:1]


def backward_unit(qs, gs, w_ref, far, scale_ref, delta_ref, refs, rows, gkv, gq_run, first, p_ref, d_ref):
    k, v = load(refs, rows, far, 0), load(refs, rows, far, HEAD)
    keys = k.shape[0]
    big = qs.shape[0]
    pair = min(big, 2 * HEAD)
    kt = k.T
    for c in range(0, big, pair):
        cols = slice(c, c + pair)
        prob = w_ref[far * keys : (far + 1) * keys, cols].astype(F32) * scale_ref[:, cols]
        dp = dot_nt(v, gs[cols, :])
        p_ref[:, cols] = prob.astype(BF16)
        d_ref[:, cols] = (prob * (dp - delta_ref[:, cols])).astype(BF16)
    gkv[:, :HEAD] = (dot(d_ref[...], qs[...]) * FACTOR).astype(BF16)
    gkv[:, HEAD:] = dot(p_ref[...], gs[...]).astype(BF16)
    more = dot(kt, d_ref[...])
    gq_run[...] = more if first is None else first[...] + more


def back_kernel(half, rows, parts, pieces, blanks, carried, new, last, qs, gs, delta_ref, *refs):
    late = is_late(half)
    refs = list(refs)
    take = lambda n: [refs.pop(0) for _ in range(n)]
    blocks = [(take(2), take(n)) for n in pieces]
    kept = take(1)[0] if last else None
    first = take(carried)[-1] if carried else None
    outs = take(new)
    gq_ref, out_ref = take(2) if last else (None, None)
    gq_run = take(1)[0]
    if last:
        copy = pltpu.make_async_copy(kept, out_ref, refs.pop())
        copy.start()
    keys = half * rows
    block = lambda out, row: outs[out].at[row * keys : (row + 1) * keys, :]
    for when in ("late", "early", "all"):
        chosen = [p for p in parts if p[0] == when]
        empty = [block(out, row) for w, out, row in blanks if w == when]
        if not chosen and not empty:
            continue

        def run(chosen=chosen, empty=empty):
            for ref in empty:
                ref[...] = jnp.zeros_like(ref)
            for n, (_, far, out, row, which) in enumerate(chosen):
                (w_ref, scale_ref), kv = blocks[which]
                backward_unit(
                    qs, gs, w_ref, far, scale_ref, delta_ref, kv, rows, block(out, row), gq_run,
                    first if n == 0 else gq_run, refs[2 * n], refs[2 * n + 1],
                )

        if when == "all":
            run()
        else:
            pl.when(late if when == "late" else jnp.logical_not(late))(run)
    if last:
        for h in range(qs.shape[0] // rows):
            g16 = (gq_run[:, h * rows : (h + 1) * rows] * FACTOR).astype(BF16)
            gq_ref[:, h * HEAD : (h + 1) * HEAD] = g16.T
        copy.wait()


def like(shape, dtype):
    return jax.ShapeDtypeStruct(shape, dtype)


def call(kernel, outs, scratch, keys, args, out_specs=None, aliases={}):
    work = 2 * keys * HEAD * HEAD * 8
    return pl.pallas_call(
        kernel,
        out_shape=outs,
        in_specs=[VMEM] * len(args),
        out_specs=out_specs or [VMEM] * len(outs),
        scratch_shapes=scratch,
        input_output_aliases=aliases,
        cost_estimate=pl.CostEstimate(flops=4 * work, bytes_accessed=1 << 20, transcendentals=work // 256),
        compiler_params=pltpu.CompilerParams(vmem_limit_bytes=30 << 20),
    )(*args)


def step(queries, key_rows, values, out_grad, span_order):
    rows, width = queries.shape
    grp_count = lax.axis_size("grp")
    blk_count = lax.axis_size("blk")
    half = grp_count // 2
    unit = half * rows
    big = width // HEAD * rows
    wide, line = like((HEAD, big), F32), like((1, big), F32)
    full = like((rows, width), BF16)
    wide_s, line_s = pltpu.VMEM((HEAD, big), F32), pltpu.VMEM((1, big), F32)

    def send(block, grp_to, blk_to):
        route = []
        for g in range(grp_count):
            for b in range(blk_count):
                to = grp_to(g)
                if to is not None:
                    route.append((g * blk_count + b, to * blk_count + blk_to(b) % blk_count))
        return lax.ppermute(block, ("grp", "blk"), route)

    same = lambda i: i
    on_chip = lambda block: send(block, same, lambda b: b ^ 1)
    off_chip = lambda block: send(block, same, lambda b: b + 1 if b % 2 else b - 1)
    ring_up = lambda block: send(block, lambda g: g // half * half + (g + 1) % half, same)
    ring_down = lambda block: send(block, lambda g: g // half * half + (g - 1) % half, same)
    across = lambda block: send(block, lambda g: (g + half) % grp_count, same)

    def scattered(block):
        slots = [block[s * rows : (s + 1) * rows] for s in range(half)]
        total = slots[-1]
        for s in range(half - 2, -1, -1):
            moved = ring_down(total)
            total = add(moved, slots[s])
        return total

    add = lambda a, b: (a.astype(F32) + b.astype(F32)).astype(BF16)
    own = lax.optimization_barrier(jnp.concatenate([key_rows, values], axis=1))

    def stacked(x):
        x = jnp.transpose(x.reshape(rows, width // HEAD, HEAD), (1, 0, 2))
        return lax.optimization_barrier(x.reshape(big, HEAD))

    qs, gs = stacked(queries), stacked(out_grad)

    def block_of(mine):
        theirs = across(mine)
        parts = [jnp.concatenate([mine, theirs], axis=0)]
        for _ in range(half - 1):
            parts.append(ring_up(parts[-1]))
        return parts

    off = off_chip(own)
    own_parts = block_of(own)
    off_parts = block_of(off)
    mate_parts = [on_chip(jnp.concatenate(own_parts, axis=0))]

    weights = like((2 * unit, big), BF16)
    scores = pltpu.VMEM((2, unit, big), F32)
    span = span_order.reshape(1, blk_count)
    forward = lambda which: functools.partial(forward_kernel, which, rows, half, blk_count)
    state = [wide, line, line, weights]
    o_run, m_own, l_run, w_own = call(forward(0), state, [scores], 2 * unit, [span, qs, *own_parts])
    o_run, m_mate, l_run, w_mate = call(
        forward(1), state, [scores], 2 * unit, [span, qs, *mate_parts, o_run, m_own, l_run]
    )
    kept, w_off, scale_own, scale_mate, scale_off, delta = call(
        functools.partial(finish_kernel, rows, half, blk_count), [full, weights, line, line, line, line],
        [wide_s, line_s, line_s, scores], 2 * unit, [span, qs, gs, *off_parts, m_own, o_run, m_mate, l_run],
    )
    saved = {
        "own": ([w_own, scale_own], own_parts), "mate": ([w_mate, scale_mate], mate_parts), "off": ([w_off, scale_off], off_parts)
    }

    def back(parts, blanks, carry, sizes, gq, last=False):
        used = list(dict.fromkeys(p[4] for p in parts))
        args = [qs, gs, delta]
        for key in used:
            args += saved[key][0] + saved[key][1]
        if last:
            args.append(kept)
        carried = list(carry) + ([] if gq is None else [gq])
        base = len(args)
        args += carried
        outs = [like(a.shape, a.dtype) for a in carry] + [like((n, 2 * HEAD), BF16) for n in sizes]
        aliases = {base + i: i for i in range(len(carry))}
        new = len(outs)
        temp = [pltpu.VMEM((unit, big), BF16)] * (2 * len(parts))
        specs = None
        if last:
            outs += [full, full]
            specs = [VMEM] * (len(outs) - 1) + [pl.BlockSpec(memory_space=pl.ANY)]
            temp = [wide_s] + temp + [pltpu.SemaphoreType.DMA]
        else:
            outs.append(wide)
            if gq is not None:
                aliases[base + len(carry)] = len(outs) - 1
        shape = tuple((when, far, out, row, used.index(key)) for when, far, out, row, key in parts)
        pieces = tuple(len(saved[key][1]) for key in used)
        kernel = functools.partial(back_kernel, half, rows, shape, pieces, blanks, len(carried), new, last)
        return call(kernel, outs, temp, unit * len(parts), args, specs, aliases)

    gef, gsf, gm, gq = back(
        [("late", 1, 0, 0, "off"), ("early", 0, 1, 0, "off"), ("early", 0, 2, 0, "mate")],
        (("early", 0, 0), ("early", 2, 1)), [], [unit, unit, 2 * unit], None,
    )
    gm, gq = back([("late", 1, 0, 1, "mate"), ("late", 0, 0, 0, "mate")], (), [gm], [], gq)
    gsf, geo, gq = back([("late", 1, 1, 0, "own"), ("late", 0, 0, 0, "off")], (("early", 1, 0),), [gsf], [unit], gq)
    gso, gq, out = back([("all", 0, 0, 0, "own")], (), [], [unit], gq, last=True)

    back_f = across(gef)
    gsf = add(gsf, back_f)
    total_f = scattered(gsf)
    ret_f = off_chip(total_f)
    mate = on_chip(gm)
    geo = add(geo, mate[unit:])
    back_o = across(geo)
    gso = gso.astype(F32) + mate[:unit].astype(F32)
    gso = (gso + back_o.astype(F32)).astype(BF16)
    final = add(scattered(gso), ret_f)
    return (out, gq, final[:, :HEAD], final[:, HEAD:])


def solution(mesh):
    spec = P(("grp", "blk"), None)
    return jax.shard_map(
        step,
        mesh=mesh,
        in_specs=(spec, spec, spec, spec, P()),
        out_specs=(spec, spec, spec, spec),
        check_vma=False,
    )
```

```python
import functools
import math

import jax
import jax.numpy as jnp
from jax import lax
from jax.experimental import pallas as pl
from jax.experimental.pallas import tpu as pltpu
from jax.sharding import PartitionSpec as P


HEAD = 128
NEG_FILL = -1e30
F32 = jnp.float32
BF16 = jnp.bfloat16
NT = (((1,), (1,)), ((), ()))
FACTOR = 1.0 / math.sqrt(HEAD)
C2 = FACTOR * math.log2(math.e)
VMEM = pl.BlockSpec(memory_space=pltpu.VMEM)


def dot(a, b):
    return jnp.dot(a, b, preferred_element_type=F32)


def dot_nt(a, b):
    return lax.dot_general(a, b, NT, preferred_element_type=F32)


def biases(half, blk_count, span_ref):
    blk = lax.axis_index("blk")
    late = lax.axis_index("grp") >= half
    step = jnp.where(lax.rem(blk, 2) == 0, 1, -1)
    span = span_ref[:1, :]
    ids = lax.broadcasted_iota(jnp.int32, span.shape, 1)
    pick = lambda b: jnp.sum(jnp.where(ids == lax.rem(b + blk_count, blk_count), span, 0), axis=1, keepdims=True)
    mine = pick(blk)
    sign = jnp.where(late, 1, -1)
    hidden = lambda other: jnp.where((pick(other) - mine) * sign > 0, 0.0, NEG_FILL)
    return hidden(blk + step), hidden(blk - step)


def is_late(half):
    return lax.axis_index("grp") >= half


def own_mask(keys, rows, idx):
    row = lax.broadcasted_iota(jnp.int32, (keys, 2 * rows), 0)
    col = lax.broadcasted_iota(jnp.int32, (keys, 2 * rows), 1)
    col = jnp.where(col >= rows, col - rows, col)
    return (row <= col) | ((row >= rows) & (row < (idx + 1) * rows))


def load(refs, rows, far, column):
    tiles = []
    for ref in refs:
        for r in range(far * rows, ref.shape[0], 2 * rows):
            tiles.append(ref[r : r + rows, column : column + HEAD])
    return jnp.concatenate(tiles, axis=0) if len(tiles) > 1 else tiles[0]


def attend_group(refs, rows, count, hidden, mask, qs, m_in, m_ref, w_ref, s_ref, finish):
    big = qs.shape[0]
    pair = min(big, 2 * HEAD)
    ks = [load(refs, rows, u, 0) for u in range(count)]
    keys = ks[0].shape[0]
    ones = jnp.ones((16, keys), BF16)
    for c in range(0, big, pair):
        cols = slice(c, c + pair)
        top = m_in[:, cols] if m_in is not None else jnp.full((1, pair), NEG_FILL, F32)
        for u, k in enumerate(ks):
            s = dot_nt(k, qs[cols, :]) * C2
            if u == 0 and mask is not None:
                s = jnp.where(mask, s, NEG_FILL)
            s_ref[u, :, cols] = s
            peak = jnp.max(s, axis=0, keepdims=True)
            if u == 0 and hidden is not None:
                peak = jnp.where(hidden < 0.0, NEG_FILL, peak)
            top = jnp.maximum(top, peak)
        m_ref[:, cols] = top
    vt = [jnp.concatenate([load(refs, rows, u, HEAD).T, ones], axis=0) for u in range(count)]
    vt = jnp.concatenate(vt, axis=1) if count > 1 else vt[0]
    for c in range(0, big, pair):
        cols = slice(c, c + pair)
        for u in range(count):
            base = m_ref[:, cols]
            if u == 0 and hidden is not None:
                base = jnp.where(hidden < 0.0, -NEG_FILL, base)
            w_ref[u * keys : (u + 1) * keys, cols] = jnp.exp2(s_ref[u, :, cols] - base).astype(BF16)
        summed = dot(vt, w_ref[: count * keys, cols])
        finish(cols, summed[:HEAD], summed[HEAD : HEAD + 1])


def attend_block(which, rows, half, blk_count, span_ref, qs, refs, before, o_run, m_run, l_run, w_ref, s_ref):
    late = is_late(half)
    o_in, m_in, l_in = before or (None, None, None)

    def finish(cols, summed, total):
        if before:
            alpha = jnp.exp2(m_in[:, cols] - m_run[:, cols])
            summed = o_in[:, cols] * alpha + summed
            total = l_in[:, cols] * alpha + total
        o_run[:, cols] = summed
        l_run[:, cols] = total

    hidden = mask = None
    if which == 0:
        mask = own_mask(half * rows, rows, lax.rem(lax.axis_index("grp"), half))
    else:
        hidden = biases(half, blk_count, span_ref)[which - 1]
    for count, on in ((2, late), (1, jnp.logical_not(late))):
        pl.when(on)(
            functools.partial(attend_group, refs, rows, count, hidden, mask, qs, m_in, m_run, w_ref, s_ref, finish)
        )


def forward_kernel(which, rows, half, blk_count, span_ref, qs, *refs):
    refs = list(refs)
    o_run, m_run, l_run, w_ref, s_ref = refs[-5:]
    before = refs[-8:-5] if which else None
    attend_block(
        which, rows, half, blk_count, span_ref, qs, refs[: -8 if which else -5], before, o_run, m_run, l_run, w_ref, s_ref
    )


def finish_kernel(rows, half, blk_count, span_ref, qs, gs, *refs):
    refs = list(refs)
    m_first, o_in, m_in, l_in, out_ref, w_ref, a_ref, b_ref, c_ref, delta_ref, o_run, m_run, l_run, s_ref = refs[-14:]
    attend_block(
        2, rows, half, blk_count, span_ref, qs, refs[:-14], (o_in, m_in, l_in), o_run, m_run, l_run, w_ref, s_ref
    )
    big = qs.shape[0]
    pair = 2 * rows
    ones = jnp.ones((8, HEAD), BF16)
    for p in range(big // pair):
        cols = slice(p * pair, (p + 1) * pair)
        inv = 1.0 / l_run[:, cols]
        a_ref[:, cols] = inv * jnp.exp2(m_first[:, cols] - m_run[:, cols])
        b_ref[:, cols] = inv * jnp.exp2(m_in[:, cols] - m_run[:, cols])
        c_ref[:, cols] = inv
        o16 = (o_run[:, cols] * inv).astype(BF16).T
        out_ref[:, 2 * p * HEAD : (2 * p + 1) * HEAD] = o16[:rows]
        out_ref[:, (2 * p + 1) * HEAD : (2 * p + 2) * HEAD] = o16[rows:]
        prod = o16.astype(F32) * gs[cols, :].astype(F32)
        high = prod.astype(BF16)
        low = (prod - high.astype(F32)).astype(BF16)
        delta_ref[:, cols] = (dot_nt(ones, high) + dot_nt(ones, low))[:1]


def backward_unit(qs, gs, w_ref, far, scale_ref, delta_ref, refs, rows, gkv, gq_run, first, p_ref, d_ref):
    k, v = load(refs, rows, far, 0), load(refs, rows, far, HEAD)
    keys = k.shape[0]
    big = qs.shape[0]
    pair = min(big, 2 * HEAD)
    kt = k.T
    for c in range(0, big, pair):
        cols = slice(c, c + pair)
        prob = w_ref[far * keys : (far + 1) * keys, cols].astype(F32) * scale_ref[:, cols]
        dp = dot_nt(v, gs[cols, :])
        p_ref[:, cols] = prob.astype(BF16)
        d_ref[:, cols] = (prob * (dp - delta_ref[:, cols])).astype(BF16)
    gkv[:, :HEAD] = (dot(d_ref[...], qs[...]) * FACTOR).astype(BF16)
    gkv[:, HEAD:] = dot(p_ref[...], gs[...]).astype(BF16)
    more = dot(kt, d_ref[...])
    gq_run[...] = more if first is None else first[...] + more


def back_kernel(half, rows, parts, pieces, blanks, carried, new, last, qs, gs, delta_ref, *refs):
    late = is_late(half)
    refs = list(refs)
    take = lambda n: [refs.pop(0) for _ in range(n)]
    blocks = [(take(2), take(n)) for n in pieces]
    kept = take(1)[0] if last else None
    first = take(carried)[-1] if carried else None
    outs = take(new)
    gq_ref, out_ref = take(2) if last else (None, None)
    gq_run = take(1)[0]
    if last:
        copy = pltpu.make_async_copy(kept, out_ref, refs.pop())
        copy.start()
    keys = half * rows
    block = lambda out, row: outs[out].at[row * keys : (row + 1) * keys, :]
    for when in ("late", "early", "all"):
        chosen = [p for p in parts if p[0] == when]
        empty = [block(out, row) for w, out, row in blanks if w == when]
        if not chosen and not empty:
            continue

        def run(chosen=chosen, empty=empty):
            for ref in empty:
                ref[...] = jnp.zeros_like(ref)
            for n, (_, far, out, row, which) in enumerate(chosen):
                (w_ref, scale_ref), kv = blocks[which]
                backward_unit(
                    qs, gs, w_ref, far, scale_ref, delta_ref, kv, rows, block(out, row), gq_run,
                    first if n == 0 else gq_run, refs[2 * n], refs[2 * n + 1],
                )

        if when == "all":
            run()
        else:
            pl.when(late if when == "late" else jnp.logical_not(late))(run)
    if last:
        for h in range(qs.shape[0] // rows):
            g16 = (gq_run[:, h * rows : (h + 1) * rows] * FACTOR).astype(BF16)
            gq_ref[:, h * HEAD : (h + 1) * HEAD] = g16.T
        copy.wait()


def like(shape, dtype):
    return jax.ShapeDtypeStruct(shape, dtype)


def call(kernel, outs, scratch, keys, args, out_specs=None, aliases={}):
    work = 2 * keys * HEAD * HEAD * 8
    return pl.pallas_call(
        kernel,
        out_shape=outs,
        in_specs=[VMEM] * len(args),
        out_specs=out_specs or [VMEM] * len(outs),
        scratch_shapes=scratch,
        input_output_aliases=aliases,
        cost_estimate=pl.CostEstimate(flops=4 * work, bytes_accessed=1 << 20, transcendentals=work // 256),
        compiler_params=pltpu.CompilerParams(vmem_limit_bytes=30 << 20),
    )(*args)


def step(queries, key_rows, values, out_grad, span_order):
    rows, width = queries.shape
    grp_count = lax.axis_size("grp")
    blk_count = lax.axis_size("blk")
    half = grp_count // 2
    unit = half * rows
    big = width // HEAD * rows
    wide, line = like((HEAD, big), F32), like((1, big), F32)
    full = like((rows, width), BF16)
    wide_s, line_s = pltpu.VMEM((HEAD, big), F32), pltpu.VMEM((1, big), F32)

    def send(block, grp_to, blk_to):
        route = []
        for g in range(grp_count):
            for b in range(blk_count):
                to = grp_to(g)
                if to is not None:
                    route.append((g * blk_count + b, to * blk_count + blk_to(b) % blk_count))
        return lax.ppermute(block, ("grp", "blk"), route)

    same = lambda i: i
    on_chip = lambda block: send(block, same, lambda b: b ^ 1)
    off_chip = lambda block: send(block, same, lambda b: b + 1 if b % 2 else b - 1)
    ring_up = lambda block: send(block, lambda g: g // half * half + (g + 1) % half, same)
    ring_down = lambda block: send(block, lambda g: g // half * half + (g - 1) % half, same)
    across = lambda block: send(block, lambda g: (g + half) % grp_count, same)

    def scattered(block, apart=False):
        slots = [block[s * rows : (s + 1) * rows] for s in range(half)]
        total = slots[-1]
        for s in range(half - 2, -1, -1):
            moved = ring_down(total)
            if s == 0 and apart:
                return slots[0], moved
            total = add(moved, slots[s])
        return total

    add = lambda a, b: (a.astype(F32) + b.astype(F32)).astype(BF16)
    own = lax.optimization_barrier(jnp.concatenate([key_rows, values], axis=1))

    def stacked(x):
        x = jnp.transpose(x.reshape(rows, width // HEAD, HEAD), (1, 0, 2))
        return lax.optimization_barrier(x.reshape(big, HEAD))

    qs, gs = stacked(queries), stacked(out_grad)
    span = lax.optimization_barrier(jnp.maximum(jnp.broadcast_to(span_order[None, :], (8, blk_count)), 0))

    def block_of(mine):
        theirs = across(mine)
        parts = [jnp.concatenate([mine, theirs], axis=0)]
        for _ in range(half - 1):
            parts.append(ring_up(parts[-1]))
        return parts

    off = off_chip(own)
    own_parts = block_of(own)
    off_parts = block_of(off)
    mate_parts = [on_chip(jnp.concatenate(own_parts, axis=0))]

    weights = like((2 * unit, big), BF16)
    scores = pltpu.VMEM((2, unit, big), F32)
    forward = lambda which: functools.partial(forward_kernel, which, rows, half, blk_count)
    state = [wide, line, line, weights]
    o_run, m_own, l_run, w_own = call(forward(0), state, [scores], 2 * unit, [span, qs, *own_parts])
    o_run, m_mate, l_run, w_mate = call(
        forward(1), state, [scores], 2 * unit, [span, qs, *mate_parts, o_run, m_own, l_run]
    )
    kept, w_off, scale_own, scale_mate, scale_off, delta = call(
        functools.partial(finish_kernel, rows, half, blk_count), [full, weights, line, line, line, line],
        [wide_s, line_s, line_s, scores], 2 * unit, [span, qs, gs, *off_parts, m_own, o_run, m_mate, l_run],
    )
    saved = {
        "own": ([w_own, scale_own], own_parts), "mate": ([w_mate, scale_mate], mate_parts), "off": ([w_off, scale_off], off_parts)
    }

    def back(parts, blanks, carry, sizes, gq, last=False):
        used = list(dict.fromkeys(p[4] for p in parts))
        args = [qs, gs, delta]
        for key in used:
            args += saved[key][0] + saved[key][1]
        if last:
            args.append(kept)
        carried = list(carry) + ([] if gq is None else [gq])
        base = len(args)
        args += carried
        outs = [like(a.shape, a.dtype) for a in carry] + [like((n, 2 * HEAD), BF16) for n in sizes]
        aliases = {base + i: i for i in range(len(carry))}
        new = len(outs)
        temp = [pltpu.VMEM((unit, big), BF16)] * (2 * len(parts))
        specs = None
        if last:
            outs += [full, full]
            specs = [VMEM] * (len(outs) - 1) + [pl.BlockSpec(memory_space=pl.ANY)]
            temp = [wide_s] + temp + [pltpu.SemaphoreType.DMA]
        else:
            outs.append(wide)
            if gq is not None:
                aliases[base + len(carry)] = len(outs) - 1
        shape = tuple((when, far, out, row, used.index(key)) for when, far, out, row, key in parts)
        pieces = tuple(len(saved[key][1]) for key in used)
        kernel = functools.partial(back_kernel, half, rows, shape, pieces, blanks, len(carried), new, last)
        return call(kernel, outs, temp, unit * len(parts), args, specs, aliases)

    gef, gsf, gm, gq = back(
        [("late", 1, 0, 0, "off"), ("early", 0, 1, 0, "off"), ("early", 0, 2, 0, "mate")],
        (("early", 0, 0), ("early", 2, 1)), [], [unit, unit, 2 * unit], None,
    )
    gm, gq = back([("late", 1, 0, 1, "mate"), ("late", 0, 0, 0, "mate")], (), [gm], [], gq)
    gsf, geo, gq = back([("late", 1, 1, 0, "own"), ("late", 0, 0, 0, "off")], (("early", 1, 0),), [gsf], [unit], gq)
    gso, gq, out = back([("all", 0, 0, 0, "own")], (), [], [unit], gq, last=True)

    back_f = across(gef)
    gsf = add(gsf, back_f)
    total_f = scattered(gsf)
    ret_f = off_chip(total_f)
    mate = on_chip(gm)
    geo = add(geo, mate[unit:])
    back_o = across(geo)
    gso = gso.astype(F32) + mate[:unit].astype(F32)
    gso = (gso + back_o.astype(F32)).astype(BF16)
    mine, moved = scattered(gso, True)

    def final(part):
        return (mine[:, part].astype(F32) + moved[:, part].astype(F32) + ret_f[:, part].astype(F32)).astype(BF16)

    return (out, gq, final(slice(0, HEAD)), final(slice(HEAD, 2 * HEAD)))


def solution(mesh):
    spec = P(("grp", "blk"), None)
    return jax.shard_map(
        step,
        mesh=mesh,
        in_specs=(spec, spec, spec, spec, P()),
        out_specs=(spec, spec, spec, spec),
        check_vma=False,
    )
```

```python
import functools
import math

import jax
import jax.numpy as jnp
from jax import lax
from jax.experimental import pallas as pl
from jax.experimental.pallas import tpu as pltpu
from jax.sharding import PartitionSpec as P


HEAD = 128
NEG_FILL = -1e30
F32 = jnp.float32
BF16 = jnp.bfloat16
NT = (((1,), (1,)), ((), ()))
FACTOR = 1.0 / math.sqrt(HEAD)
C2 = FACTOR * math.log2(math.e)
VMEM = pl.BlockSpec(memory_space=pltpu.VMEM)


def dot(a, b):
    return jnp.dot(a, b, preferred_element_type=F32)


def dot_nt(a, b):
    return lax.dot_general(a, b, NT, preferred_element_type=F32)


def biases(half, blk_count, span_ref):
    blk = lax.axis_index("blk")
    late = lax.axis_index("grp") >= half
    step = jnp.where(lax.rem(blk, 2) == 0, 1, -1)
    span = span_ref[:1, :]
    ids = lax.broadcasted_iota(jnp.int32, span.shape, 1)
    pick = lambda b: jnp.sum(jnp.where(ids == lax.rem(b + blk_count, blk_count), span, 0), axis=1, keepdims=True)
    mine = pick(blk)
    sign = jnp.where(late, 1, -1)
    hidden = lambda other: jnp.where((pick(other) - mine) * sign > 0, 0.0, NEG_FILL)
    return hidden(blk + step), hidden(blk - step)


def is_late(half):
    return lax.axis_index("grp") >= half


def own_mask(keys, rows, idx):
    row = lax.broadcasted_iota(jnp.int32, (keys, 2 * rows), 0)
    col = lax.broadcasted_iota(jnp.int32, (keys, 2 * rows), 1)
    col = jnp.where(col >= rows, col - rows, col)
    return (row <= col) | ((row >= rows) & (row < (idx + 1) * rows))


def load(refs, rows, far, column):
    tiles = []
    for ref in refs:
        for r in range(far * rows, ref.shape[0], 2 * rows):
            tiles.append(ref[r : r + rows, column : column + HEAD])
    return jnp.concatenate(tiles, axis=0) if len(tiles) > 1 else tiles[0]


def attend_group(refs, rows, count, hidden, mask, qs, m_in, m_ref, w_ref, s_ref, finish):
    big = qs.shape[0]
    pair = min(big, 2 * HEAD)
    ks = [load(refs, rows, u, 0) for u in range(count)]
    keys = ks[0].shape[0]
    ones = jnp.ones((16, keys), BF16)
    for c in range(0, big, pair):
        cols = slice(c, c + pair)
        top = m_in[:, cols] if m_in is not None else jnp.full((1, pair), NEG_FILL, F32)
        for u, k in enumerate(ks):
            s = dot_nt(k, qs[cols, :]) * C2
            if u == 0 and mask is not None:
                s = jnp.where(mask, s, NEG_FILL)
            s_ref[u, :, cols] = s
            peak = jnp.max(s, axis=0, keepdims=True)
            if u == 0 and hidden is not None:
                peak = jnp.where(hidden < 0.0, NEG_FILL, peak)
            top = jnp.maximum(top, peak)
        m_ref[:, cols] = top
    vt = [jnp.concatenate([load(refs, rows, u, HEAD).T, ones], axis=0) for u in range(count)]
    vt = jnp.concatenate(vt, axis=1) if count > 1 else vt[0]
    for c in range(0, big, pair):
        cols = slice(c, c + pair)
        for u in range(count):
            base = m_ref[:, cols]
            if u == 0 and hidden is not None:
                base = jnp.where(hidden < 0.0, -NEG_FILL, base)
            w_ref[u * keys : (u + 1) * keys, cols] = jnp.exp2(s_ref[u, :, cols] - base).astype(BF16)
        summed = dot(vt, w_ref[: count * keys, cols])
        finish(cols, summed[:HEAD], summed[HEAD : HEAD + 1])


def attend_block(which, rows, half, blk_count, span_ref, qs, refs, before, o_run, m_run, l_run, w_ref, s_ref):
    late = is_late(half)
    o_in, m_in, l_in = before or (None, None, None)

    def finish(cols, summed, total):
        if before:
            alpha = jnp.exp2(m_in[:, cols] - m_run[:, cols])
            summed = o_in[:, cols] * alpha + summed
            total = l_in[:, cols] * alpha + total
        o_run[:, cols] = summed
        l_run[:, cols] = total

    hidden = mask = None
    if which == 0:
        mask = own_mask(half * rows, rows, lax.rem(lax.axis_index("grp"), half))
    else:
        hidden = biases(half, blk_count, span_ref)[which - 1]
    for count, on in ((2, late), (1, jnp.logical_not(late))):
        pl.when(on)(
            functools.partial(attend_group, refs, rows, count, hidden, mask, qs, m_in, m_run, w_ref, s_ref, finish)
        )


def forward_kernel(which, rows, half, blk_count, span_ref, qs, *refs):
    refs = list(refs)
    o_run, m_run, l_run, w_ref, s_ref = refs[-5:]
    before = refs[-8:-5] if which else None
    attend_block(
        which, rows, half, blk_count, span_ref, qs, refs[: -8 if which else -5], before, o_run, m_run, l_run, w_ref, s_ref
    )


def finish_kernel(rows, half, blk_count, span_ref, qs, gs, *refs):
    refs = list(refs)
    m_first, o_in, m_in, l_in, out_ref, w_ref, a_ref, b_ref, c_ref, delta_ref, o_run, m_run, l_run, s_ref = refs[-14:]
    attend_block(
        2, rows, half, blk_count, span_ref, qs, refs[:-14], (o_in, m_in, l_in), o_run, m_run, l_run, w_ref, s_ref
    )
    big = qs.shape[0]
    pair = 2 * rows
    ones = jnp.ones((8, HEAD), BF16)
    for p in range(big // pair):
        cols = slice(p * pair, (p + 1) * pair)
        inv = 1.0 / l_run[:, cols]
        a_ref[:, cols] = inv * jnp.exp2(m_first[:, cols] - m_run[:, cols])
        b_ref[:, cols] = inv * jnp.exp2(m_in[:, cols] - m_run[:, cols])
        c_ref[:, cols] = inv
        o16 = (o_run[:, cols] * inv).astype(BF16).T
        out_ref[:, 2 * p * HEAD : (2 * p + 1) * HEAD] = o16[:rows]
        out_ref[:, (2 * p + 1) * HEAD : (2 * p + 2) * HEAD] = o16[rows:]
        prod = o16.astype(F32) * gs[cols, :].astype(F32)
        high = prod.astype(BF16)
        low = (prod - high.astype(F32)).astype(BF16)
        delta_ref[:, cols] = (dot_nt(ones, high) + dot_nt(ones, low))[:1]


def backward_unit(qs, gs, w_ref, far, scale_ref, delta_ref, refs, rows, gkv, gq_run, first, p_ref, d_ref):
    k, v = load(refs, rows, far, 0), load(refs, rows, far, HEAD)
    keys = k.shape[0]
    big = qs.shape[0]
    pair = min(big, 2 * HEAD)
    kt = k.T
    for c in range(0, big, pair):
        cols = slice(c, c + pair)
        prob = w_ref[far * keys : (far + 1) * keys, cols].astype(F32) * scale_ref[:, cols]
        dp = dot_nt(v, gs[cols, :])
        p_ref[:, cols] = prob.astype(BF16)
        d_ref[:, cols] = (prob * (dp - delta_ref[:, cols])).astype(BF16)
    gkv[:, :HEAD] = (dot(d_ref[...], qs[...]) * FACTOR).astype(BF16)
    gkv[:, HEAD:] = dot(p_ref[...], gs[...]).astype(BF16)
    more = dot(kt, d_ref[...])
    gq_run[...] = more if first is None else first[...] + more


def back_kernel(half, rows, parts, pieces, blanks, carried, new, last, qs, gs, delta_ref, *refs):
    late = is_late(half)
    refs = list(refs)
    take = lambda n: [refs.pop(0) for _ in range(n)]
    blocks = [(take(2), take(n)) for n in pieces]
    kept = take(1)[0] if last else None
    held = take(carried)
    first = held[-1] if held else None
    outs = take(new)
    gq_ref, out_ref = take(2) if last else (None, None)
    gq_run = take(1)[0]
    if last:
        copy = pltpu.make_async_copy(kept, out_ref, refs.pop())
        copy.start()
    keys = half * rows
    block = lambda out, row: outs[out].at[row * keys : (row + 1) * keys, :]
    for when in ("late", "early", "all"):
        chosen = [p for p in parts if p[0] == when]
        empty = [block(out, row) for w, out, row in blanks if w == when]
        kept_on = list(zip(held, outs[: len(held) - 1] + [gq_run])) if when == "early" and not last and held else []
        if not chosen and not empty and not kept_on:
            continue

        def run(chosen=chosen, empty=empty, kept_on=kept_on):
            for old, ref in kept_on:
                ref[...] = old[...]
            for ref in empty:
                ref[...] = jnp.zeros_like(ref)
            for n, (_, far, out, row, which) in enumerate(chosen):
                (w_ref, scale_ref), kv = blocks[which]
                backward_unit(
                    qs, gs, w_ref, far, scale_ref, delta_ref, kv, rows, block(out, row), gq_run,
                    first if n == 0 else gq_run, refs[2 * n], refs[2 * n + 1],
                )

        if when == "all":
            run()
        else:
            pl.when(late if when == "late" else jnp.logical_not(late))(run)
    if last:
        for h in range(qs.shape[0] // rows):
            g16 = (gq_run[:, h * rows : (h + 1) * rows] * FACTOR).astype(BF16)
            gq_ref[:, h * HEAD : (h + 1) * HEAD] = g16.T
        copy.wait()


def like(shape, dtype):
    return jax.ShapeDtypeStruct(shape, dtype)


def call(kernel, outs, scratch, keys, args, out_specs=None, aliases={}):
    work = 2 * keys * HEAD * HEAD * 8
    return pl.pallas_call(
        kernel,
        out_shape=outs,
        in_specs=[VMEM] * len(args),
        out_specs=out_specs or [VMEM] * len(outs),
        scratch_shapes=scratch,
        input_output_aliases=aliases,
        cost_estimate=pl.CostEstimate(flops=4 * work, bytes_accessed=1 << 20, transcendentals=work // 256),
        compiler_params=pltpu.CompilerParams(vmem_limit_bytes=30 << 20),
    )(*args)


def step(queries, key_rows, values, out_grad, span_order):
    rows, width = queries.shape
    grp_count = lax.axis_size("grp")
    blk_count = lax.axis_size("blk")
    half = grp_count // 2
    unit = half * rows
    big = width // HEAD * rows
    wide, line = like((HEAD, big), F32), like((1, big), F32)
    full = like((rows, width), BF16)
    wide_s, line_s = pltpu.VMEM((HEAD, big), F32), pltpu.VMEM((1, big), F32)

    def send(block, grp_to, blk_to):
        route = []
        for g in range(grp_count):
            for b in range(blk_count):
                to = grp_to(g)
                if to is not None:
                    route.append((g * blk_count + b, to * blk_count + blk_to(b) % blk_count))
        return lax.ppermute(block, ("grp", "blk"), route)

    same = lambda i: i
    on_chip = lambda block: send(block, same, lambda b: b ^ 1)
    off_chip = lambda block: send(block, same, lambda b: b + 1 if b % 2 else b - 1)
    ring_up = lambda block: send(block, lambda g: g // half * half + (g + 1) % half, same)
    ring_down = lambda block: send(block, lambda g: g // half * half + (g - 1) % half, same)
    across = lambda block: send(block, lambda g: (g + half) % grp_count, same)

    def scattered(block, apart=False):
        slots = [block[s * rows : (s + 1) * rows] for s in range(half)]
        total = slots[-1]
        for s in range(half - 2, -1, -1):
            moved = ring_down(total)
            if s == 0 and apart:
                return slots[0], moved
            total = add(moved, slots[s])
        return total

    add = lambda a, b: (a.astype(F32) + b.astype(F32)).astype(BF16)
    own = lax.optimization_barrier(jnp.concatenate([key_rows, values], axis=1))

    def stacked(x):
        x = jnp.transpose(x.reshape(rows, width // HEAD, HEAD), (1, 0, 2))
        return lax.optimization_barrier(x.reshape(big, HEAD))

    qs, gs = stacked(queries), stacked(out_grad)
    span = lax.optimization_barrier(jnp.maximum(jnp.broadcast_to(span_order[None, :], (8, blk_count)), 0))

    def block_of(mine):
        theirs = across(mine)
        parts = [jnp.concatenate([mine, theirs], axis=0)]
        for _ in range(half - 1):
            parts.append(ring_up(parts[-1]))
        return parts

    off = off_chip(own)
    own_parts = block_of(own)
    off_parts = block_of(off)
    mate_parts = [on_chip(jnp.concatenate(own_parts, axis=0))]

    weights = like((2 * unit, big), BF16)
    scores = pltpu.VMEM((2, unit, big), F32)
    forward = lambda which: functools.partial(forward_kernel, which, rows, half, blk_count)
    state = [wide, line, line, weights]
    o_run, m_own, l_run, w_own = call(forward(0), state, [scores], 2 * unit, [span, qs, *own_parts])
    o_run, m_mate, l_run, w_mate = call(
        forward(1), state, [scores], 2 * unit, [span, qs, *mate_parts, o_run, m_own, l_run]
    )
    kept, w_off, scale_own, scale_mate, scale_off, delta = call(
        functools.partial(finish_kernel, rows, half, blk_count), [full, weights, line, line, line, line],
        [wide_s, line_s, line_s, scores], 2 * unit, [span, qs, gs, *off_parts, m_own, o_run, m_mate, l_run],
    )
    saved = {
        "own": ([w_own, scale_own], own_parts), "mate": ([w_mate, scale_mate], mate_parts), "off": ([w_off, scale_off], off_parts)
    }

    def back(parts, blanks, carry, sizes, gq, last=False):
        used = list(dict.fromkeys(p[4] for p in parts))
        args = [qs, gs, delta]
        for key in used:
            args += saved[key][0] + saved[key][1]
        if last:
            args.append(kept)
        carried = list(carry) + ([] if gq is None else [gq])
        base = len(args)
        args += carried
        outs = [like(a.shape, a.dtype) for a in carry] + [like((n, 2 * HEAD), BF16) for n in sizes]
        aliases = {base + i: i for i in range(len(carry))}
        new = len(outs)
        temp = [pltpu.VMEM((unit, big), BF16)] * (2 * len(parts))
        specs = None
        if last:
            outs += [full, full]
            specs = [VMEM] * (len(outs) - 1) + [pl.BlockSpec(memory_space=pl.ANY)]
            temp = [wide_s] + temp + [pltpu.SemaphoreType.DMA]
        else:
            outs.append(wide)
            if gq is not None:
                aliases[base + len(carry)] = len(outs) - 1
        shape = tuple((when, far, out, row, used.index(key)) for when, far, out, row, key in parts)
        pieces = tuple(len(saved[key][1]) for key in used)
        kernel = functools.partial(back_kernel, half, rows, shape, pieces, blanks, len(carried), new, last)
        return call(kernel, outs, temp, unit * len(parts), args, specs, aliases)

    gef, gsf, gm, gq = back(
        [("late", 1, 0, 0, "off"), ("early", 0, 1, 0, "off"), ("early", 0, 2, 0, "mate")],
        (("early", 0, 0), ("early", 2, 1)), [], [unit, unit, 2 * unit], None,
    )
    gm, gq = back([("late", 1, 0, 1, "mate"), ("late", 0, 0, 0, "mate")], (), [gm], [], gq)
    gsf, geo, gq = back([("late", 1, 1, 0, "own"), ("late", 0, 0, 0, "off")], (("early", 1, 0),), [gsf], [unit], gq)
    gso, gq, out = back([("all", 0, 0, 0, "own")], (), [], [unit], gq, last=True)

    back_f = across(gef)
    gsf = add(gsf, back_f)
    total_f = scattered(gsf)
    ret_f = off_chip(total_f)
    mate = on_chip(gm)
    geo = add(geo, mate[unit:])
    back_o = across(geo)
    gso = gso.astype(F32) + mate[:unit].astype(F32)
    gso = (gso + back_o.astype(F32)).astype(BF16)
    mine, moved = scattered(gso, True)

    def final(part):
        return (mine[:, part].astype(F32) + moved[:, part].astype(F32) + ret_f[:, part].astype(F32)).astype(BF16)

    return (out, gq, final(slice(0, HEAD)), final(slice(HEAD, 2 * HEAD)))


def solution(mesh):
    spec = P(("grp", "blk"), None)
    return jax.shard_map(
        step,
        mesh=mesh,
        in_specs=(spec, spec, spec, spec, P()),
        out_specs=(spec, spec, spec, spec),
        check_vma=False,
    )
```

```python
import functools
import math

import jax
import jax.numpy as jnp
from jax import lax
from jax.experimental import pallas as pl
from jax.experimental.pallas import tpu as pltpu
from jax.sharding import PartitionSpec as P


HEAD = 128
NEG_FILL = -1e30
F32 = jnp.float32
BF16 = jnp.bfloat16
NT = (((1,), (1,)), ((), ()))
FACTOR = 1.0 / math.sqrt(HEAD)
C2 = FACTOR * math.log2(math.e)
VMEM = pl.BlockSpec(memory_space=pltpu.VMEM)


def dot(a, b):
    return jnp.dot(a, b, preferred_element_type=F32)


def dot_nt(a, b):
    return lax.dot_general(a, b, NT, preferred_element_type=F32)


def biases(half, blk_count, span_ref):
    blk = lax.axis_index("blk")
    late = lax.axis_index("grp") >= half
    step = jnp.where(lax.rem(blk, 2) == 0, 1, -1)
    span = span_ref[:1, :]
    ids = lax.broadcasted_iota(jnp.int32, span.shape, 1)
    pick = lambda b: jnp.sum(jnp.where(ids == lax.rem(b + blk_count, blk_count), span, 0), axis=1, keepdims=True)
    mine = pick(blk)
    sign = jnp.where(late, 1, -1)
    hidden = lambda other: jnp.where((pick(other) - mine) * sign > 0, 0.0, NEG_FILL)
    return hidden(blk + step), hidden(blk - step)


def is_late(half):
    return lax.axis_index("grp") >= half


def own_mask(keys, rows, idx):
    row = lax.broadcasted_iota(jnp.int32, (keys, 2 * rows), 0)
    col = lax.broadcasted_iota(jnp.int32, (keys, 2 * rows), 1)
    col = jnp.where(col >= rows, col - rows, col)
    return (row <= col) | ((row >= rows) & (row < (idx + 1) * rows))


def load(refs, rows, far, column):
    tiles = []
    for ref in refs:
        for r in range(far * rows, ref.shape[0], 2 * rows):
            tiles.append(ref[r : r + rows, column : column + HEAD])
    return jnp.concatenate(tiles, axis=0) if len(tiles) > 1 else tiles[0]


def attend_group(refs, rows, count, hidden, mask, qs, m_in, m_ref, w_ref, s_ref, finish):
    big = qs.shape[0]
    pair = min(big, 2 * HEAD)
    ks = [load(refs, rows, u, 0) for u in range(count)]
    keys = ks[0].shape[0]
    ones = jnp.ones((16, keys), BF16)
    for c in range(0, big, pair):
        cols = slice(c, c + pair)
        top = m_in[:, cols] if m_in is not None else jnp.full((1, pair), NEG_FILL, F32)
        for u, k in enumerate(ks):
            s = dot_nt(k, qs[cols, :]) * C2
            if u == 0 and mask is not None:
                s = jnp.where(mask, s, NEG_FILL)
            s_ref[u, :, cols] = s
            peak = jnp.max(s, axis=0, keepdims=True)
            if u == 0 and hidden is not None:
                peak = jnp.where(hidden < 0.0, NEG_FILL, peak)
            top = jnp.maximum(top, peak)
        m_ref[:, cols] = top
    vt = [jnp.concatenate([load(refs, rows, u, HEAD).T, ones], axis=0) for u in range(count)]
    vt = jnp.concatenate(vt, axis=1) if count > 1 else vt[0]
    for c in range(0, big, pair):
        cols = slice(c, c + pair)
        for u in range(count):
            base = m_ref[:, cols]
            if u == 0 and hidden is not None:
                base = jnp.where(hidden < 0.0, -NEG_FILL, base)
            w_ref[u * keys : (u + 1) * keys, cols] = jnp.exp2(s_ref[u, :, cols] - base).astype(BF16)
        summed = dot(vt, w_ref[: count * keys, cols])
        finish(cols, summed[:HEAD], summed[HEAD : HEAD + 1])


def attend_block(which, rows, half, blk_count, span_ref, qs, refs, before, o_run, m_run, l_run, w_ref, s_ref):
    late = is_late(half)
    o_in, m_in, l_in = before or (None, None, None)

    def finish(cols, summed, total):
        if before:
            alpha = jnp.exp2(m_in[:, cols] - m_run[:, cols])
            summed = o_in[:, cols] * alpha + summed
            total = l_in[:, cols] * alpha + total
        o_run[:, cols] = summed
        l_run[:, cols] = total

    hidden = mask = None
    if which == 0:
        mask = own_mask(half * rows, rows, lax.rem(lax.axis_index("grp"), half))
    else:
        hidden = biases(half, blk_count, span_ref)[which - 1]
    for count, on in ((2, late), (1, jnp.logical_not(late))):
        pl.when(on)(
            functools.partial(attend_group, refs, rows, count, hidden, mask, qs, m_in, m_run, w_ref, s_ref, finish)
        )


def forward_kernel(which, rows, half, blk_count, span_ref, qs, *refs):
    refs = list(refs)
    o_run, m_run, l_run, w_ref, s_ref = refs[-5:]
    before = refs[-8:-5] if which else None
    attend_block(
        which, rows, half, blk_count, span_ref, qs, refs[: -8 if which else -5], before, o_run, m_run, l_run, w_ref, s_ref
    )


def finish_kernel(rows, half, blk_count, span_ref, qs, gs, *refs):
    refs = list(refs)
    m_first, o_in, m_in, l_in, out_ref, w_ref, a_ref, b_ref, c_ref, delta_ref, o_run, m_run, l_run, s_ref = refs[-14:]
    attend_block(
        2, rows, half, blk_count, span_ref, qs, refs[:-14], (o_in, m_in, l_in), o_run, m_run, l_run, w_ref, s_ref
    )
    big = qs.shape[0]
    pair = 2 * rows
    ones = jnp.ones((8, HEAD), BF16)
    for p in range(big // pair):
        cols = slice(p * pair, (p + 1) * pair)
        inv = 1.0 / l_run[:, cols]
        a_ref[:, cols] = inv * jnp.exp2(m_first[:, cols] - m_run[:, cols])
        b_ref[:, cols] = inv * jnp.exp2(m_in[:, cols] - m_run[:, cols])
        c_ref[:, cols] = inv
        o16 = (o_run[:, cols] * inv).astype(BF16).T
        out_ref[:, 2 * p * HEAD : (2 * p + 1) * HEAD] = o16[:rows]
        out_ref[:, (2 * p + 1) * HEAD : (2 * p + 2) * HEAD] = o16[rows:]
        prod = o16.astype(F32) * gs[cols, :].astype(F32)
        high = prod.astype(BF16)
        low = (prod - high.astype(F32)).astype(BF16)
        delta_ref[:, cols] = (dot_nt(ones, high) + dot_nt(ones, low))[:1]


def backward_unit(qs, gs, w_ref, far, scale_ref, delta_ref, refs, rows, gkv, gq_run, first, p_ref, d_ref):
    k, v = load(refs, rows, far, 0), load(refs, rows, far, HEAD)
    keys = k.shape[0]
    big = qs.shape[0]
    pair = min(big, 2 * HEAD)
    kt = k.T
    for c in range(0, big, pair):
        cols = slice(c, c + pair)
        prob = w_ref[far * keys : (far + 1) * keys, cols].astype(F32) * scale_ref[:, cols]
        dp = dot_nt(v, gs[cols, :])
        p_ref[:, cols] = prob.astype(BF16)
        d_ref[:, cols] = (prob * (dp - delta_ref[:, cols])).astype(BF16)
    gkv[:, :HEAD] = (dot(d_ref[...], qs[...]) * FACTOR).astype(BF16)
    gkv[:, HEAD:] = dot(p_ref[...], gs[...]).astype(BF16)
    more = dot(kt, d_ref[...])
    gq_run[...] = more if first is None else first[...] + more


def back_kernel(half, rows, parts, pieces, blanks, carried, new, last, qs, gs, delta_ref, *refs):
    late = is_late(half)
    refs = list(refs)
    take = lambda n: [refs.pop(0) for _ in range(n)]
    blocks = [(take(2), take(n)) for n in pieces]
    kept = take(1)[0] if last else None
    held = take(carried)
    first = held[-1] if held else None
    outs = take(new)
    gq_ref, out_ref = take(2) if last else (None, None)
    gq_run = take(1)[0]
    if last:
        copy = pltpu.make_async_copy(kept, out_ref, refs.pop())
        copy.start()
    keys = half * rows
    block = lambda out, row: outs[out].at[row * keys : (row + 1) * keys, :]
    for when in ("late", "early", "all"):
        chosen = [p for p in parts if p[0] == when]
        empty = [block(out, row) for w, out, row in blanks if w == when]
        kept_on = list(zip(held, outs[: len(held) - 1] + [gq_run])) if when == "early" and held else []
        if not chosen and not empty and not kept_on:
            continue

        def run(chosen=chosen, empty=empty, kept_on=kept_on):
            for old, ref in kept_on:
                ref[...] = old[...]
            for ref in empty:
                ref[...] = jnp.zeros_like(ref)
            for n, (_, far, out, row, which) in enumerate(chosen):
                (w_ref, scale_ref), kv = blocks[which]
                backward_unit(
                    qs, gs, w_ref, far, scale_ref, delta_ref, kv, rows, block(out, row), gq_run,
                    first if n == 0 else gq_run, refs[2 * n], refs[2 * n + 1],
                )

        if when == "all":
            run()
        else:
            pl.when(late if when == "late" else jnp.logical_not(late))(run)
    if last:
        for h in range(qs.shape[0] // rows):
            g16 = (gq_run[:, h * rows : (h + 1) * rows] * FACTOR).astype(BF16)
            gq_ref[:, h * HEAD : (h + 1) * HEAD] = g16.T
        copy.wait()


def like(shape, dtype):
    return jax.ShapeDtypeStruct(shape, dtype)


def call(kernel, outs, scratch, keys, args, out_specs=None, aliases={}):
    work = 2 * keys * HEAD * HEAD * 8
    return pl.pallas_call(
        kernel,
        out_shape=outs,
        in_specs=[VMEM] * len(args),
        out_specs=out_specs or [VMEM] * len(outs),
        scratch_shapes=scratch,
        input_output_aliases=aliases,
        cost_estimate=pl.CostEstimate(flops=4 * work, bytes_accessed=1 << 20, transcendentals=work // 256),
        compiler_params=pltpu.CompilerParams(vmem_limit_bytes=30 << 20),
    )(*args)


def step(queries, key_rows, values, out_grad, span_order):
    rows, width = queries.shape
    grp_count = lax.axis_size("grp")
    blk_count = lax.axis_size("blk")
    half = grp_count // 2
    unit = half * rows
    big = width // HEAD * rows
    wide, line = like((HEAD, big), F32), like((1, big), F32)
    full = like((rows, width), BF16)
    wide_s, line_s = pltpu.VMEM((HEAD, big), F32), pltpu.VMEM((1, big), F32)

    def send(block, grp_to, blk_to):
        route = []
        for g in range(grp_count):
            for b in range(blk_count):
                to = grp_to(g)
                if to is not None:
                    route.append((g * blk_count + b, to * blk_count + blk_to(b) % blk_count))
        return lax.ppermute(block, ("grp", "blk"), route)

    same = lambda i: i
    on_chip = lambda block: send(block, same, lambda b: b ^ 1)
    off_chip = lambda block: send(block, same, lambda b: b + 1 if b % 2 else b - 1)
    ring_up = lambda block: send(block, lambda g: g // half * half + (g + 1) % half, same)
    ring_down = lambda block: send(block, lambda g: g // half * half + (g - 1) % half, same)
    across = lambda block: send(block, lambda g: (g + half) % grp_count, same)

    def scattered(block, apart=False):
        slots = [block[s * rows : (s + 1) * rows] for s in range(half)]
        total = slots[-1]
        for s in range(half - 2, -1, -1):
            moved = ring_down(total)
            if s == 0 and apart:
                return slots[0], moved
            total = add(moved, slots[s])
        return total

    add = lambda a, b: (a.astype(F32) + b.astype(F32)).astype(BF16)
    own = lax.optimization_barrier(jnp.concatenate([key_rows, values], axis=1))

    def stacked(x):
        x = jnp.transpose(x.reshape(rows, width // HEAD, HEAD), (1, 0, 2))
        return lax.optimization_barrier(x.reshape(big, HEAD))

    qs, gs = stacked(queries), stacked(out_grad)
    span = lax.optimization_barrier(jnp.maximum(jnp.broadcast_to(span_order[None, :], (8, blk_count)), 0))

    def block_of(mine):
        theirs = across(mine)
        parts = [jnp.concatenate([mine, theirs], axis=0)]
        for _ in range(half - 1):
            parts.append(ring_up(parts[-1]))
        return parts

    off = off_chip(own)
    own_parts = block_of(own)
    off_parts = block_of(off)
    mate_parts = [on_chip(jnp.concatenate(own_parts, axis=0))]

    weights = like((2 * unit, big), BF16)
    scores = pltpu.VMEM((2, unit, big), F32)
    forward = lambda which: functools.partial(forward_kernel, which, rows, half, blk_count)
    state = [wide, line, line, weights]
    o_run, m_own, l_run, w_own = call(forward(0), state, [scores], 2 * unit, [span, qs, *own_parts])
    o_run, m_mate, l_run, w_mate = call(
        forward(1), state, [scores], 2 * unit, [span, qs, *mate_parts, o_run, m_own, l_run]
    )
    kept, w_off, scale_own, scale_mate, scale_off, delta = call(
        functools.partial(finish_kernel, rows, half, blk_count), [full, weights, line, line, line, line],
        [wide_s, line_s, line_s, scores], 2 * unit, [span, qs, gs, *off_parts, m_own, o_run, m_mate, l_run],
    )
    saved = {
        "own": ([w_own, scale_own], own_parts), "mate": ([w_mate, scale_mate], mate_parts), "off": ([w_off, scale_off], off_parts)
    }

    def back(parts, blanks, carry, sizes, gq, last=False):
        used = list(dict.fromkeys(p[4] for p in parts))
        args = [qs, gs, delta]
        for key in used:
            args += saved[key][0] + saved[key][1]
        if last:
            args.append(kept)
        carried = list(carry) + ([] if gq is None else [gq])
        base = len(args)
        args += carried
        outs = [like(a.shape, a.dtype) for a in carry] + [like((n, 2 * HEAD), BF16) for n in sizes]
        aliases = {base + i: i for i in range(len(carry))}
        new = len(outs)
        temp = [pltpu.VMEM((unit, big), BF16)] * (2 * len(parts))
        specs = None
        if last:
            outs += [full, full]
            specs = [VMEM] * (len(outs) - 1) + [pl.BlockSpec(memory_space=pl.ANY)]
            temp = [wide_s] + temp + [pltpu.SemaphoreType.DMA]
        else:
            outs.append(wide)
            if gq is not None:
                aliases[base + len(carry)] = len(outs) - 1
        shape = tuple((when, far, out, row, used.index(key)) for when, far, out, row, key in parts)
        pieces = tuple(len(saved[key][1]) for key in used)
        kernel = functools.partial(back_kernel, half, rows, shape, pieces, blanks, len(carried), new, last)
        return call(kernel, outs, temp, unit * len(parts), args, specs, aliases)

    gef, gsf, gm, gq = back(
        [("late", 1, 0, 0, "off"), ("early", 0, 1, 0, "off"), ("early", 0, 2, 0, "mate")],
        (("early", 0, 0), ("early", 2, 1)), [], [unit, unit, 2 * unit], None,
    )
    gsf, gm, gso, gq = back(
        [("late", 0, 0, 0, "off"), ("late", 1, 1, 1, "mate"), ("late", 0, 1, 0, "mate"), ("early", 0, 2, 0, "own")],
        (), [gsf, gm], [unit], gq,
    )
    geo, gq = back([("late", 1, 0, 0, "own")], (("early", 0, 0),), [], [unit], gq)
    gso, gq, out = back([("late", 0, 0, 0, "own")], (), [gso], [], gq, last=True)

    back_1 = across(gef[rows:])
    back_0 = across(gef[:rows])
    total_f = gsf[unit - rows :].astype(F32) + back_1[unit - 2 * rows :].astype(F32)
    for s in range(half - 2, -1, -1):
        moved = ring_down(total_f.astype(BF16))
        more = back_1[(s - 1) * rows : s * rows] if s > 0 else back_0
        total_f = moved.astype(F32) + gsf[s * rows : (s + 1) * rows].astype(F32) + more.astype(F32)
    total_f = total_f.astype(BF16)
    ret_f = off_chip(total_f)
    mate = on_chip(gm)
    geo = add(geo, mate[unit:])
    back_o = across(geo)
    gso = gso.astype(F32) + mate[:unit].astype(F32)
    gso = (gso + back_o.astype(F32)).astype(BF16)
    mine, moved = scattered(gso, True)

    def final(part):
        return (mine[:, part].astype(F32) + moved[:, part].astype(F32) + ret_f[:, part].astype(F32)).astype(BF16)

    return (out, gq, final(slice(0, HEAD)), final(slice(HEAD, 2 * HEAD)))


def solution(mesh):
    spec = P(("grp", "blk"), None)
    return jax.shard_map(
        step,
        mesh=mesh,
        in_specs=(spec, spec, spec, spec, P()),
        out_specs=(spec, spec, spec, spec),
        check_vma=False,
    )
```

```python
import functools
import math

import jax
import jax.numpy as jnp
from jax import lax
from jax.experimental import pallas as pl
from jax.experimental.pallas import tpu as pltpu
from jax.sharding import PartitionSpec as P


HEAD = 128
NEG_FILL = -1e30
F32 = jnp.float32
BF16 = jnp.bfloat16
NT = (((1,), (1,)), ((), ()))
FACTOR = 1.0 / math.sqrt(HEAD)
C2 = FACTOR * math.log2(math.e)
VMEM = pl.BlockSpec(memory_space=pltpu.VMEM)


def dot(a, b):
    return jnp.dot(a, b, preferred_element_type=F32)


def dot_nt(a, b):
    return lax.dot_general(a, b, NT, preferred_element_type=F32)


def biases(half, blk_count, span_ref):
    blk = lax.axis_index("blk")
    late = lax.axis_index("grp") >= half
    step = jnp.where(lax.rem(blk, 2) == 0, 1, -1)
    span = span_ref[:1, :]
    ids = lax.broadcasted_iota(jnp.int32, span.shape, 1)
    pick = lambda b: jnp.sum(jnp.where(ids == lax.rem(b + blk_count, blk_count), span, 0), axis=1, keepdims=True)
    mine = pick(blk)
    sign = jnp.where(late, 1, -1)
    hidden = lambda other: jnp.where((pick(other) - mine) * sign > 0, 0.0, NEG_FILL)
    return hidden(blk + step), hidden(blk - step)


def is_late(half):
    return lax.axis_index("grp") >= half


def own_mask(keys, rows, idx):
    row = lax.broadcasted_iota(jnp.int32, (keys, 2 * rows), 0)
    col = lax.broadcasted_iota(jnp.int32, (keys, 2 * rows), 1)
    col = jnp.where(col >= rows, col - rows, col)
    return (row <= col) | ((row >= rows) & (row < (idx + 1) * rows))


def load(refs, rows, far, column):
    tiles = []
    for ref in refs:
        for r in range(far * rows, ref.shape[0], 2 * rows):
            tiles.append(ref[r : r + rows, column : column + HEAD])
    return jnp.concatenate(tiles, axis=0) if len(tiles) > 1 else tiles[0]


def attend_group(refs, rows, count, hidden, mask, qs, m_in, m_ref, w_ref, s_ref, finish):
    big = qs.shape[0]
    pair = min(big, 2 * HEAD)
    ks = []
    for u in range(count):
        scaled = load(refs, rows, u, 0).astype(F32) * C2
        high = scaled.astype(BF16)
        ks.append(jnp.concatenate([high, (scaled - high.astype(F32)).astype(BF16)], axis=1))
    keys = ks[0].shape[0]
    ones = jnp.ones((16, keys), BF16)
    for c in range(0, big, pair):
        cols = slice(c, c + pair)
        top = m_in[:, cols] if m_in is not None else jnp.full((1, pair), NEG_FILL, F32)
        q2 = jnp.concatenate([qs[cols, :], qs[cols, :]], axis=1)
        for u, k in enumerate(ks):
            s = dot_nt(k, q2)
            if u == 0 and mask is not None:
                s = jnp.where(mask, s, NEG_FILL)
            s_ref[u, :, cols] = s
            peak = jnp.max(s, axis=0, keepdims=True)
            if u == 0 and hidden is not None:
                peak = jnp.where(hidden < 0.0, NEG_FILL, peak)
            top = jnp.maximum(top, peak)
        m_ref[:, cols] = top
    vt = [jnp.concatenate([load(refs, rows, u, HEAD).T, ones], axis=0) for u in range(count)]
    vt = jnp.concatenate(vt, axis=1) if count > 1 else vt[0]
    for c in range(0, big, pair):
        cols = slice(c, c + pair)
        for u in range(count):
            base = m_ref[:, cols]
            if u == 0 and hidden is not None:
                base = jnp.where(hidden < 0.0, -NEG_FILL, base)
            w_ref[u * keys : (u + 1) * keys, cols] = jnp.exp2(s_ref[u, :, cols] - base).astype(BF16)
        summed = dot(vt, w_ref[: count * keys, cols])
        finish(cols, summed[:HEAD], summed[HEAD : HEAD + 1])


def attend_block(which, rows, half, blk_count, span_ref, qs, refs, before, o_run, m_run, l_run, w_ref, s_ref):
    late = is_late(half)
    o_in, m_in, l_in = before or (None, None, None)

    def finish(cols, summed, total):
        if before:
            alpha = jnp.exp2(m_in[:, cols] - m_run[:, cols])
            summed = o_in[:, cols] * alpha + summed
            total = l_in[:, cols] * alpha + total
        o_run[:, cols] = summed
        l_run[:, cols] = total

    hidden = mask = None
    if which == 0:
        mask = own_mask(half * rows, rows, lax.rem(lax.axis_index("grp"), half))
    else:
        hidden = biases(half, blk_count, span_ref)[which - 1]
    for count, on in ((2, late), (1, jnp.logical_not(late))):
        pl.when(on)(
            functools.partial(attend_group, refs, rows, count, hidden, mask, qs, m_in, m_run, w_ref, s_ref, finish)
        )


def forward_kernel(which, rows, half, blk_count, span_ref, qs, *refs):
    refs = list(refs)
    o_run, m_run, l_run, w_ref, s_ref = refs[-5:]
    before = refs[-8:-5] if which else None
    attend_block(
        which, rows, half, blk_count, span_ref, qs, refs[: -8 if which else -5], before, o_run, m_run, l_run, w_ref, s_ref
    )


def finish_kernel(rows, half, blk_count, span_ref, qs, gs, *refs):
    refs = list(refs)
    m_first, o_in, m_in, l_in, out_ref, w_ref, a_ref, b_ref, c_ref, delta_ref, o_run, m_run, l_run, s_ref = refs[-14:]
    attend_block(
        2, rows, half, blk_count, span_ref, qs, refs[:-14], (o_in, m_in, l_in), o_run, m_run, l_run, w_ref, s_ref
    )
    big = qs.shape[0]
    pair = 2 * rows
    ones = jnp.ones((8, HEAD), BF16)
    for p in range(big // pair):
        cols = slice(p * pair, (p + 1) * pair)
        inv = 1.0 / l_run[:, cols]
        a_ref[:, cols] = inv * jnp.exp2(m_first[:, cols] - m_run[:, cols])
        b_ref[:, cols] = inv * jnp.exp2(m_in[:, cols] - m_run[:, cols])
        c_ref[:, cols] = inv
        o16 = (o_run[:, cols] * inv).astype(BF16).T
        out_ref[:, 2 * p * HEAD : (2 * p + 1) * HEAD] = o16[:rows]
        out_ref[:, (2 * p + 1) * HEAD : (2 * p + 2) * HEAD] = o16[rows:]
        prod = o16.astype(F32) * gs[cols, :].astype(F32)
        high = prod.astype(BF16)
        low = (prod - high.astype(F32)).astype(BF16)
        delta_ref[:, cols] = (dot_nt(ones, high) + dot_nt(ones, low))[:1]


def backward_unit(qs, gs, w_ref, far, scale_ref, delta_ref, refs, rows, gkv, gq_run, first, p_ref, d_ref):
    k, v = load(refs, rows, far, 0), load(refs, rows, far, HEAD)
    keys = k.shape[0]
    big = qs.shape[0]
    pair = min(big, 2 * HEAD)
    kt = k.T
    for c in range(0, big, pair):
        cols = slice(c, c + pair)
        prob = w_ref[far * keys : (far + 1) * keys, cols].astype(F32) * scale_ref[:, cols]
        dp = dot_nt(v, gs[cols, :])
        p_ref[:, cols] = prob.astype(BF16)
        d_ref[:, cols] = (prob * (dp - delta_ref[:, cols])).astype(BF16)
    gkv[:, :HEAD] = (dot(d_ref[...], qs[...]) * FACTOR).astype(BF16)
    gkv[:, HEAD:] = dot(p_ref[...], gs[...]).astype(BF16)
    more = dot(kt, d_ref[...])
    gq_run[...] = more if first is None else first[...] + more


def back_kernel(half, rows, parts, pieces, blanks, carried, new, last, qs, gs, delta_ref, *refs):
    late = is_late(half)
    refs = list(refs)
    take = lambda n: [refs.pop(0) for _ in range(n)]
    blocks = [(take(2), take(n)) for n in pieces]
    kept = take(1)[0] if last else None
    held = take(carried)
    first = held[-1] if held else None
    outs = take(new)
    gq_ref, out_ref = take(2) if last else (None, None)
    gq_run = take(1)[0]
    if last:
        copy = pltpu.make_async_copy(kept, out_ref, refs.pop())
        copy.start()
    keys = half * rows
    block = lambda out, row: outs[out].at[row * keys : (row + 1) * keys, :]
    for when in ("late", "early", "all"):
        chosen = [p for p in parts if p[0] == when]
        empty = [block(out, row) for w, out, row in blanks if w == when]
        kept_on = list(zip(held, outs[: len(held) - 1] + [gq_run])) if when == "early" and held else []
        if not chosen and not empty and not kept_on:
            continue

        def run(chosen=chosen, empty=empty, kept_on=kept_on):
            for old, ref in kept_on:
                ref[...] = old[...]
            for ref in empty:
                ref[...] = jnp.zeros_like(ref)
            for n, (_, far, out, row, which) in enumerate(chosen):
                (w_ref, scale_ref), kv = blocks[which]
                backward_unit(
                    qs, gs, w_ref, far, scale_ref, delta_ref, kv, rows, block(out, row), gq_run,
                    first if n == 0 else gq_run, refs[2 * n], refs[2 * n + 1],
                )

        if when == "all":
            run()
        else:
            pl.when(late if when == "late" else jnp.logical_not(late))(run)
    if last:
        for h in range(qs.shape[0] // rows):
            g16 = (gq_run[:, h * rows : (h + 1) * rows] * FACTOR).astype(BF16)
            gq_ref[:, h * HEAD : (h + 1) * HEAD] = g16.T
        copy.wait()


def like(shape, dtype):
    return jax.ShapeDtypeStruct(shape, dtype)


def call(kernel, outs, scratch, keys, args, out_specs=None, aliases={}):
    work = 2 * keys * HEAD * HEAD * 8
    return pl.pallas_call(
        kernel,
        out_shape=outs,
        in_specs=[VMEM] * len(args),
        out_specs=out_specs or [VMEM] * len(outs),
        scratch_shapes=scratch,
        input_output_aliases=aliases,
        cost_estimate=pl.CostEstimate(flops=4 * work, bytes_accessed=1 << 20, transcendentals=work // 256),
        compiler_params=pltpu.CompilerParams(vmem_limit_bytes=30 << 20),
    )(*args)


def step(queries, key_rows, values, out_grad, span_order):
    rows, width = queries.shape
    grp_count = lax.axis_size("grp")
    blk_count = lax.axis_size("blk")
    half = grp_count // 2
    unit = half * rows
    big = width // HEAD * rows
    wide, line = like((HEAD, big), F32), like((1, big), F32)
    full = like((rows, width), BF16)
    wide_s, line_s = pltpu.VMEM((HEAD, big), F32), pltpu.VMEM((1, big), F32)

    def send(block, grp_to, blk_to):
        route = []
        for g in range(grp_count):
            for b in range(blk_count):
                to = grp_to(g)
                if to is not None:
                    route.append((g * blk_count + b, to * blk_count + blk_to(b) % blk_count))
        return lax.ppermute(block, ("grp", "blk"), route)

    same = lambda i: i
    on_chip = lambda block: send(block, same, lambda b: b ^ 1)
    off_chip = lambda block: send(block, same, lambda b: b + 1 if b % 2 else b - 1)
    ring_up = lambda block: send(block, lambda g: g // half * half + (g + 1) % half, same)
    ring_down = lambda block: send(block, lambda g: g // half * half + (g - 1) % half, same)
    across = lambda block: send(block, lambda g: (g + half) % grp_count, same)

    def scattered(block, apart=False):
        slots = [block[s * rows : (s + 1) * rows] for s in range(half)]
        total = slots[-1]
        for s in range(half - 2, -1, -1):
            moved = ring_down(total)
            if s == 0 and apart:
                return slots[0], moved
            total = add(moved, slots[s])
        return total

    add = lambda a, b: (a.astype(F32) + b.astype(F32)).astype(BF16)
    own = lax.optimization_barrier(jnp.concatenate([key_rows, values], axis=1))

    def stacked(x):
        x = jnp.transpose(x.reshape(rows, width // HEAD, HEAD), (1, 0, 2))
        return lax.optimization_barrier(x.reshape(big, HEAD))

    qs, gs = stacked(queries), stacked(out_grad)
    span = lax.optimization_barrier(jnp.maximum(jnp.broadcast_to(span_order[None, :], (8, blk_count)), 0))

    def block_of(mine):
        theirs = across(mine)
        parts = [jnp.concatenate([mine, theirs], axis=0)]
        for _ in range(half - 1):
            parts.append(ring_up(parts[-1]))
        return parts

    off = off_chip(own)
    own_parts = block_of(own)
    off_parts = block_of(off)
    mate_parts = [on_chip(jnp.concatenate(own_parts, axis=0))]

    weights = like((2 * unit, big), BF16)
    scores = pltpu.VMEM((2, unit, big), F32)
    forward = lambda which: functools.partial(forward_kernel, which, rows, half, blk_count)
    state = [wide, line, line, weights]
    o_run, m_own, l_run, w_own = call(forward(0), state, [scores], 2 * unit, [span, qs, *own_parts])
    o_run, m_mate, l_run, w_mate = call(
        forward(1), state, [scores], 2 * unit, [span, qs, *mate_parts, o_run, m_own, l_run]
    )
    kept, w_off, scale_own, scale_mate, scale_off, delta = call(
        functools.partial(finish_kernel, rows, half, blk_count), [full, weights, line, line, line, line],
        [wide_s, line_s, line_s, scores], 2 * unit, [span, qs, gs, *off_parts, m_own, o_run, m_mate, l_run],
    )
    saved = {
        "own": ([w_own, scale_own], own_parts), "mate": ([w_mate, scale_mate], mate_parts), "off": ([w_off, scale_off], off_parts)
    }

    def back(parts, blanks, carry, sizes, gq, last=False):
        used = list(dict.fromkeys(p[4] for p in parts))
        args = [qs, gs, delta]
        for key in used:
            args += saved[key][0] + saved[key][1]
        if last:
            args.append(kept)
        carried = list(carry) + ([] if gq is None else [gq])
        base = len(args)
        args += carried
        outs = [like(a.shape, a.dtype) for a in carry] + [like((n, 2 * HEAD), BF16) for n in sizes]
        aliases = {base + i: i for i in range(len(carry))}
        new = len(outs)
        temp = [pltpu.VMEM((unit, big), BF16)] * (2 * len(parts))
        specs = None
        if last:
            outs += [full, full]
            specs = [VMEM] * (len(outs) - 1) + [pl.BlockSpec(memory_space=pl.ANY)]
            temp = [wide_s] + temp + [pltpu.SemaphoreType.DMA]
        else:
            outs.append(wide)
            if gq is not None:
                aliases[base + len(carry)] = len(outs) - 1
        shape = tuple((when, far, out, row, used.index(key)) for when, far, out, row, key in parts)
        pieces = tuple(len(saved[key][1]) for key in used)
        kernel = functools.partial(back_kernel, half, rows, shape, pieces, blanks, len(carried), new, last)
        return call(kernel, outs, temp, unit * len(parts), args, specs, aliases)

    gef, gsf, gm, gq = back(
        [("late", 1, 0, 0, "off"), ("early", 0, 1, 0, "off"), ("early", 0, 2, 0, "mate")],
        (("early", 0, 0), ("early", 2, 1)), [], [unit, unit, 2 * unit], None,
    )
    gsf, gm, gso, gq = back(
        [("late", 0, 0, 0, "off"), ("late", 1, 1, 1, "mate"), ("late", 0, 1, 0, "mate"), ("early", 0, 2, 0, "own")],
        (), [gsf, gm], [unit], gq,
    )
    geo, gq = back([("late", 1, 0, 0, "own")], (("early", 0, 0),), [], [unit], gq)
    gso, gq, out = back([("late", 0, 0, 0, "own")], (), [gso], [], gq, last=True)

    back_1 = across(gef[rows:])
    back_0 = across(gef[:rows])
    total_f = gsf[unit - rows :].astype(F32) + back_1[unit - 2 * rows :].astype(F32)
    for s in range(half - 2, -1, -1):
        moved = ring_down(total_f.astype(BF16))
        more = back_1[(s - 1) * rows : s * rows] if s > 0 else back_0
        total_f = moved.astype(F32) + gsf[s * rows : (s + 1) * rows].astype(F32) + more.astype(F32)
    total_f = total_f.astype(BF16)
    ret_f = off_chip(total_f)
    mate = on_chip(gm)
    geo = add(geo, mate[unit:])
    back_o = across(geo)
    gso = gso.astype(F32) + mate[:unit].astype(F32)
    gso = (gso + back_o.astype(F32)).astype(BF16)
    mine, moved = scattered(gso, True)

    def final(part):
        return (mine[:, part].astype(F32) + moved[:, part].astype(F32) + ret_f[:, part].astype(F32)).astype(BF16)

    return (out, gq, final(slice(0, HEAD)), final(slice(HEAD, 2 * HEAD)))


def solution(mesh):
    spec = P(("grp", "blk"), None)
    return jax.shard_map(
        step,
        mesh=mesh,
        in_specs=(spec, spec, spec, spec, P()),
        out_specs=(spec, spec, spec, spec),
        check_vma=False,
    )
```
